32 devices in a mesh: dp: 2 (over x), mp: 16 (over z, y, core).
Axes of the slice: x: 2, y: 2, z: 4, core: 2. Of those that a mesh axis runs over, the one named last changes fastest.
Arguments:
- inputs: bfloat16 [8192, 256], P('mp', 'dp'), may hold values from -6 to 6
- cotangent: bfloat16 [8192, 256], P('mp', 'dp'), may hold values from -6 to 6
- w_up: bfloat16 [4096, 4096], P('mp'), may hold values from -0.1875 to 0.1875
- w_down: bfloat16 [4096, 4096], P('mp'), may hold values from -0.125 to 0.125
- col_up: int32 [4096], P('mp'), may hold values from 0 to 15, as said below
- row_down: int32 [4096], P('mp'), may hold values from 0 to 15, as said below
- owner_up: int32 [4096, 1], P('mp'), may hold values from 0 to 1; in each aligned block of 256 rows (0 to 255, 256 to 511, ...) at most 160 rows name the same one
- owner_down: int32 [4096, 1], P('mp'), may hold values from 0 to 1; in each aligned block of 256 rows (0 to 255, 256 to 511, ...) at most 160 rows name the same one
Outputs:
- active: bfloat16 [16384, 256], P('mp', 'dp')
- input_grad: bfloat16 [8192, 256], P('mp', 'dp')
- grad_up: bfloat16 [5120, 4096], P(('dp', 'mp'))
- grad_down: bfloat16 [5120, 4096], P(('dp', 'mp'))
The draws below stay inside these ranges and needn't reach their ends.
Inputs may be any that keep to these rules, and one draw needn't show every extreme that they name: `col_up`: within each list of 256 entries of one index of mp, the 2 entries of each block row r (positions 2 * r to 2 * r + 1) are different block columns. `row_down`: within each list of 256 entries of one index of mp, the 2 entries of each block column r are different block rows. `owner_up`: within the 256 entries of each index of mp no index of dp appears more than 160 times, and some index of dp appears exactly 160 times. `owner_down`: within the 256 entries of each index of mp no index of dp appears more than 160 times, and some index of dp appears exactly 160 times.
All inputs are finite; a program needn't handle non-finite values.
Results may differ from the reference program's by a relative error of at most 0.0059.
Values may be sent and summed in bfloat16 or wider, within the bound.
No kernel may reach another device: no remote copies, remote signals or barrier semaphores. Data moves between devices by JAX's collectives and lax.ppermute only.
A program may use at most 128 MiB of HBM per device.

```python
import math
import jax
import jax.numpy as jnp
import numpy as np
from jax import lax

D = 8192
BS = 64
FBLK = 16
KB = 2
FF = 16384
NB = 256
CAP = 160
TOKENS = 256
N_DP = 2
N_MP = 16


def block_columns(key):
    row_total = N_MP * (D // BS)
    scores = jax.random.randint(key, (row_total, FBLK), 0, 1 << 20, dtype=jnp.int32) * FBLK
    scores = scores + jnp.arange(FBLK, dtype=jnp.int32)[None, :]
    order = jnp.argsort(scores, axis=1, stable=True)
    return order[:, :KB].reshape(row_total * KB).astype(jnp.int32)


def draw_col_up(key, part):
    return block_columns(jax.random.fold_in(key, 11))


def draw_row_down(key, part):
    return block_columns(jax.random.fold_in(key, 23))


def level_of(stream_key, shape, shards, smallest, top_value):
    level = 1.0
    for position, blocks in shards:
        heights = jax.random.uniform(jax.random.fold_in(jax.random.fold_in(stream_key, 6), position), (blocks,), jnp.float32, smallest / len(shards), top_value / len(shards))
        level = level * jnp.repeat(jnp.exp(heights), shape[position] // blocks).reshape((-1,) + (1,) * (len(shape) - 1 - position))
    return level


def deal_out(own_key, own, number, rows, count, top, limit, slope):
    ranking = jax.random.permutation(own_key, count)
    heavy_load, common = portions_of(count, rows * top, limit, slope, True), portions_of(count, rows * top, limit, slope, False)
    places = jnp.arange(count)

    def named(sizes, rotation):
        used = int((sizes > 0).sum())
        fixed = max(1, used // 4)
        shifted = fixed + (places - fixed + rotation * (used - fixed)) % max(1, count - fixed)
        return jnp.zeros((count,), jnp.int32).at[ranking[jnp.where(places < fixed, places, shifted)]].set(jnp.asarray(sizes, jnp.int32))

    sizes = jnp.where(number % 4 == 0, named(heavy_load, number // 4), named(common, number - number // 4 - 1))
    mixed = jax.random.permutation(jax.random.fold_in(own, 3), count)
    donor, taker = mixed[0:count // 2 * 2:2], mixed[1:count // 2 * 2:2]
    slack = jnp.minimum(sizes[donor] - 1, limit - sizes[taker]) // 2
    slack = jnp.where((donor == ranking[0]) | (taker == ranking[0]) | (sizes[taker] == 0), 0, jnp.maximum(slack, 0))
    shifted = jax.random.randint(jax.random.fold_in(own, 4), (count // 2,), 0, 1 << 20) % (slack + 1)
    sizes = sizes.at[donor].add(-shifted).at[taker].add(shifted)
    items = jnp.searchsorted(jnp.cumsum(sizes), jnp.arange(rows * top), side="right").astype(jnp.int32)
    grid = items.reshape(top, rows).T
    grid = grid[jax.random.permutation(jax.random.fold_in(own, 1), rows)]
    rotation = jax.random.randint(jax.random.fold_in(own, 2), (rows, 1), 0, top)
    return jnp.take_along_axis(grid, (jnp.arange(top)[None, :] + rotation) % top, axis=1)


def portions_of(count, total, reach, skew, full):
    loads = [(1 << 20) // math.isqrt(grade ** skew) + 1 for grade in range(1, count + 1)]
    largest = reach if full else min(reach, max(-(-total // count), total * loads[0] // sum(loads)))
    least = 1 if total - largest >= count - 1 else 0
    counts, surplus = [largest] + [least] * (count - 1), total - largest - least * (count - 1)
    while surplus > 0:
        free = [i for i in range(1, count) if counts[i] < largest] or [i for i in range(1, count) if counts[i] < reach]
        mass, budget = sum([loads[i] for i in free]), surplus
        for i in free:
            extra = min(reach - counts[i], max(1, budget * loads[i] // mass), surplus)
            counts[i] = counts[i] + extra
            surplus = surplus - extra
    return np.array(counts)


def centred(key, dims, deviation, bound, split=(), held_as=jnp.bfloat16):
    array = deviation * jax.random.normal(key, dims, jnp.float32)
    if split:
        array = array * level_of(key, dims, split, -0.22, 0.18)
    return jnp.clip(array, -bound, bound).astype(held_as)


def setup_inputs(seed: int = 0) -> dict:
    seeds = jax.random.split(jax.random.key(seed), 9)
    inputs = centred(seeds[0], (D, TOKENS), 1.0, 6.0, ((0, 16), (1, 2)))
    cotangent = centred(seeds[1], (D, TOKENS), 1.0, 6.0, ((0, 16), (1, 2)))
    w_up = centred(seeds[2], (N_MP * NB, BS * BS), (D * KB // FBLK) ** -0.5, 0.1875, ((0, 16),))
    w_down = centred(seeds[3], (N_MP * NB, BS * BS), (FF * KB // FBLK) ** -0.5, 0.125, ((0, 16),))
    col_up = draw_col_up(jax.random.fold_in(seeds[8], 71), 0)
    row_down = draw_row_down(jax.random.fold_in(seeds[8], 71), 0)
    owner_up_keys = jax.random.split(jax.random.fold_in(seeds[6], 1), (N_MP * NB) // NB)
    owner_up_turns = jax.random.permutation(jax.random.fold_in(seeds[6], 3), (N_MP * NB) // NB)
    owner_up = jax.vmap(lambda own, number: deal_out(jax.random.fold_in(seeds[6], 2), own, number, NB, N_DP, 1, CAP, 2))(owner_up_keys, owner_up_turns).reshape((N_MP * NB, 1))
    owner_down_keys = jax.random.split(jax.random.fold_in(seeds[7], 1), (N_MP * NB) // NB)
    owner_down_turns = jax.random.permutation(jax.random.fold_in(seeds[7], 3), (N_MP * NB) // NB)
    owner_down = jax.vmap(lambda own, number: deal_out(jax.random.fold_in(seeds[7], 2), own, number, NB, N_DP, 1, CAP, 2))(owner_down_keys, owner_down_turns).reshape((N_MP * NB, 1))
    return {"inputs": inputs, "cotangent": cotangent, "w_up": w_up, "w_down": w_down, "col_up": col_up, "row_down": row_down, "owner_up": owner_up, "owner_down": owner_down}


def gelu_slope(value):
    scale = 0.7978845608028654
    cubic = 0.044715
    inner = scale * (value + cubic * value * value * value)
    tanh_part = jnp.tanh(inner)
    return 0.5 * (1.0 + tanh_part) + 0.5 * value * (1.0 - tanh_part * tanh_part) * scale * (1.0 + 3.0 * cubic * value * value)


def owner_slots(owner, parties):
    owner = owner[:, 0]
    table = (owner[:, None] == jnp.arange(parties, dtype=jnp.int32)[None, :]).astype(jnp.int32)
    before = jnp.cumsum(table, axis=0, dtype=jnp.int32) - table
    slot = jnp.sum(before * table, axis=1, dtype=jnp.int32)
    return owner, slot


def group_sum(parts):
    rounded = parts.astype(jnp.bfloat16)
    rounded = lax.optimization_barrier(rounded)
    return jnp.sum(rounded.astype(jnp.float32), axis=0).astype(jnp.bfloat16)


def reference(inputs, cotangent, w_up, w_down, col_up, row_down, owner_up, owner_down):
    row_blocks = D // BS
    tokens = inputs.shape[1]
    group = tokens // N_DP
    features = inputs.astype(jnp.float32).reshape(row_blocks, BS, tokens)
    upstream = cotangent.astype(jnp.float32).reshape(row_blocks, BS, tokens)
    up_blocks = w_up.reshape(N_MP, row_blocks, KB, BS, BS)
    down_blocks = w_down.reshape(N_MP, row_blocks, KB, BS, BS)
    up_cols = col_up.reshape(N_MP, NB)
    down_rows = row_down.reshape(N_MP, NB)
    up_owner = owner_up.reshape(N_MP, NB, 1)
    down_owner = owner_down.reshape(N_MP, NB, 1)
    device_ids = jnp.arange(N_MP, dtype=jnp.int32)

    def device_step(carry, inputs_one):
        grads_in, up_out, down_out = carry
        w_one, w_two, columns, rows_of, own_up, own_down, index = inputs_one
        w_one = w_one.astype(jnp.float32)
        w_two = w_two.astype(jnp.float32)
        terms = jnp.einsum("rqkm,rks->rqms", w_one, features).reshape(NB, BS, tokens)
        hidden = jnp.zeros((FBLK, BS, tokens), jnp.float32).at[columns].add(terms)
        active = jax.nn.gelu(hidden, approximate=True).astype(jnp.bfloat16)
        back_terms = jnp.einsum("rqkm,rms->rqks", w_two, upstream).reshape(NB, BS, tokens)
        upper = jnp.zeros((FBLK, BS, tokens), jnp.float32).at[rows_of].add(back_terms)
        slope_grad = (upper * gelu_slope(hidden)).astype(jnp.bfloat16)
        chosen_grad = slope_grad.astype(jnp.float32)[columns].reshape(row_blocks, KB, BS, tokens)
        grads_in = grads_in + jnp.einsum("rqkm,rqms->rks", w_one, chosen_grad)
        chosen_act = active.astype(jnp.float32)[rows_of].reshape(row_blocks, KB, BS, tokens)
        parts_up = jnp.einsum("rkgs,rqmgs->grqkm", features.reshape(row_blocks, BS, N_DP, group),
                              chosen_grad.reshape(row_blocks, KB, BS, N_DP, group))
        parts_down = jnp.einsum("rqkgs,rmgs->grqkm", chosen_act.reshape(row_blocks, KB, BS, N_DP, group),
                                upstream.reshape(row_blocks, BS, N_DP, group))
        sum_up = group_sum(parts_up).reshape(NB, BS * BS)
        sum_down = group_sum(parts_down).reshape(NB, BS * BS)
        owner_a, slot_a = owner_slots(own_up, N_DP)
        owner_b, slot_b = owner_slots(own_down, N_DP)
        target_a = (owner_a * N_MP + index) * CAP + slot_a
        target_b = (owner_b * N_MP + index) * CAP + slot_b
        up_out = up_out.at[target_a].set(sum_up)
        down_out = down_out.at[target_b].set(sum_down)
        return (grads_in, up_out, down_out), active

    start = (jnp.zeros((row_blocks, BS, tokens), jnp.float32),
             jnp.zeros((N_DP * N_MP * CAP, BS * BS), jnp.bfloat16),
             jnp.zeros((N_DP * N_MP * CAP, BS * BS), jnp.bfloat16))
    carry, actives = lax.scan(device_step, start,
                              (up_blocks, down_blocks, up_cols, down_rows, up_owner, down_owner, device_ids))
    grads_in, up_out, down_out = carry
    active_all = actives.reshape(FF, tokens)
    input_grad = grads_in.reshape(D, tokens).astype(jnp.bfloat16)
    return (active_all, input_grad, up_out, down_out)
```

```python
import functools
import jax
import jax.numpy as jnp
from jax import lax
from jax.experimental import pallas as pl
from jax.experimental.pallas import tpu as pltpu
from jax.sharding import PartitionSpec as P

BS = 64
FBLK = 16
KB = 2
GROUP = 16
RELAYOUT = 32
PITCH = BS + 1
VMEM = pltpu.VMEM
SMEM = pltpu.SMEM
ANY = pl.ANY
BF = jnp.bfloat16
F32 = jnp.float32


def swap(value, axis, mask):
    size = lax.axis_size(axis)
    return lax.ppermute(value, axis, [(i, i ^ mask) for i in range(size)])


def relayout_kernel(blocks, up_ref, down_ref, up_out, down_out, low, high):
    lane = lax.broadcasted_iota(jnp.int32, (BS, 2 * BS), 1) < BS
    for src, out in ((up_ref, up_out), (down_ref, down_out)):
        for a in range(BS // 2):
            tile = src[:, a * 2 * BS : (a + 1) * 2 * BS].astype(F32)
            turned = pltpu.roll(tile, BS, 1)
            low[pl.ds(2 * a, blocks, stride=PITCH), :] = tile
            low[pl.ds(2 * a + 1, blocks, stride=PITCH), :] = turned
            high[pl.ds(2 * a, blocks, stride=PITCH), :] = turned
            high[pl.ds(2 * a + 1, blocks, stride=PITCH), :] = tile
        for r in range(blocks // KB):
            first = low[2 * r * PITCH : 2 * r * PITCH + BS, :]
            second = high[(2 * r + 1) * PITCH : (2 * r + 1) * PITCH + BS, :]
            out[r * BS : (r + 1) * BS, :] = jnp.where(lane, first, second).astype(BF)


def relayout(w_up, w_down):
    total = w_up.shape[0]
    blocks = RELAYOUT
    row = pl.BlockSpec((blocks, BS * BS), lambda i: (i, 0))
    tiles = pl.BlockSpec((blocks * BS // KB, KB * BS), lambda i: (i, 0))
    shape = jax.ShapeDtypeStruct((total * BS // KB, KB * BS), BF)
    return pl.pallas_call(
        functools.partial(relayout_kernel, blocks),
        grid=(total // blocks,),
        in_specs=[row, row],
        out_specs=[tiles, tiles],
        out_shape=[shape, shape],
        scratch_shapes=[VMEM((blocks * PITCH, 2 * BS), F32)] * 2,
        cost_estimate=pl.CostEstimate(flops=0, bytes_accessed=14 << 20, transcendentals=0),
        name="relayout",
    )(w_up, w_down)


def slots_kernel(me_ref, up_ref, down_ref, up_tab, down_tab):
    group = me_ref[0]
    total = up_ref.shape[0]
    pad = up_tab.shape[0]

    def body(e, carry):
        a, b = carry
        up_tab[a] = e
        down_tab[b] = e
        a = a + (up_ref[e] == group).astype(jnp.int32)
        b = b + (down_ref[e] == group).astype(jnp.int32)
        return a, b

    a, b = lax.fori_loop(0, total, body, (jnp.int32(0), jnp.int32(0)))

    def rest_up(t, carry):
        up_tab[t] = -1
        return carry

    def rest_down(t, carry):
        down_tab[t] = -1
        return carry

    lax.fori_loop(a, pad, rest_up, 0)
    lax.fori_loop(b, pad, rest_down, 0)


def slots(group, owner_up, owner_down):
    total = owner_up.shape[0]
    shape = jax.ShapeDtypeStruct((total + 8,), jnp.int32)
    spec = pl.BlockSpec(memory_space=SMEM)
    return pl.pallas_call(
        slots_kernel,
        in_specs=[spec] * 3,
        out_specs=[spec] * 2,
        out_shape=[shape] * 2,
        cost_estimate=pl.CostEstimate(flops=0, bytes_accessed=1 << 20, transcendentals=0),
        name="slots",
    )(group, owner_up, owner_down)


def gelu_slope(value):
    scale = 0.7978845608028654
    cubic = 0.044715
    inner = scale * (value + cubic * value * value * value)
    tanh_part = jnp.tanh(inner)
    gate = 0.5 * (1.0 + tanh_part)
    slope = gate + 0.5 * value * (1.0 - tanh_part * tanh_part) * scale * (
        1.0 + 3.0 * cubic * value * value
    )
    return value * gate, slope


def add_blocks(place, where_ref, w_ref, x_refs, acc, rows, is_up):
    per = rows // BS
    zero = jnp.zeros((BS, acc.shape[1]), BF)
    width = acc.shape[1]
    done = 0
    for x_ref in x_refs:
        chunks = x_ref.shape[0] // rows

        def body(i, carry, x_ref=x_ref, done=done):
            start = place[done + i] * per
            for rr in range(per):
                r = start + rr
                w = w_ref[pl.ds(pl.multiple_of(r * BS, BS), BS), :]
                x = x_ref[pl.ds(pl.multiple_of(i * rows + rr * BS, BS), BS), :]
                if is_up:
                    t = lax.dot_general(
                        w, x, (((0,), (0,)), ((), ())), preferred_element_type=F32
                    )
                    parts = [t[q * BS : (q + 1) * BS, :] for q in range(KB)]
                else:
                    right = jnp.concatenate(
                        [
                            jnp.concatenate([x, zero], axis=1),
                            jnp.concatenate([zero, x], axis=1),
                        ],
                        axis=0,
                    )
                    t = jnp.dot(w, right, preferred_element_type=F32)
                    parts = [t[:, q * width : (q + 1) * width] for q in range(KB)]
                for q in range(KB):
                    to = pl.ds(pl.multiple_of(where_ref[KB * r + q] * BS, BS), BS)
                    acc[to, :] += parts[q]
            return carry

        lax.fori_loop(0, chunks, body, 0)
        done += chunks


def hidden_kernel(rows, is_up, count, first, last, *refs):
    place, where_ref, w_ref = refs[:3]
    x_refs = refs[3 : 3 + count]
    rest = list(refs[3 + count :])
    acc_in = None if first else rest.pop(0)
    hidden = rest.pop(0) if last else None
    if last:
        both, acc = rest
    else:
        (acc,) = rest
    acc[...] = jnp.zeros_like(acc) if first else acc_in[...]
    add_blocks(place, where_ref, w_ref, x_refs, acc, rows, is_up)
    if last:
        ff = acc.shape[0]

        def body(i, carry):
            at = pl.multiple_of(i * BS, BS)
            value, slope = gelu_slope(hidden[pl.ds(at, BS), :])
            both[pl.ds(at, BS), :] = value.astype(BF)
            both[pl.ds(ff + at, BS), :] = (acc[pl.ds(at, BS), :] * slope).astype(BF)
            return carry

        lax.fori_loop(0, ff // BS, body, 0)


def hidden_sum(rows, is_up, place, where, w, pieces, acc=None, hidden=None):
    ff, tokens = FBLK * BS, pieces[0].shape[1]
    smem = pl.BlockSpec(memory_space=SMEM)
    vmem = pl.BlockSpec(memory_space=VMEM)
    more = [x for x in (acc, hidden) if x is not None]
    if hidden is None:
        out, scratch = jax.ShapeDtypeStruct((ff, tokens), F32), []
    else:
        out, scratch = jax.ShapeDtypeStruct((2 * ff, tokens), BF), [VMEM((ff, tokens), F32)]
    return pl.pallas_call(
        functools.partial(
            hidden_kernel, rows, is_up, len(pieces), acc is None, hidden is not None
        ),
        in_specs=[smem, smem] + [vmem] * (1 + len(pieces) + len(more)),
        out_specs=vmem,
        out_shape=out,
        scratch_shapes=scratch,
        compiler_params=pltpu.CompilerParams(vmem_limit_bytes=24 << 20),
        cost_estimate=pl.CostEstimate(
            flops=1 << 29, bytes_accessed=6 << 20, transcendentals=0
        ),
        name=("hidden" if is_up else "upper") + ("" if hidden is None else "_last"),
    )(place, where, w, *pieces, *more)


def input_grad_kernel(rows, place, col_ref, w_ref, both_ref, out):
    per = rows // BS
    chunks = out.shape[0] // rows
    base = both_ref.shape[0] // 2

    def body(i, carry):
        start = place[i] * per
        for rr in range(per):
            r = start + rr
            w = w_ref[pl.ds(pl.multiple_of(r * BS, BS), BS), :]
            parts = [
                both_ref[pl.ds(pl.multiple_of(base + col_ref[KB * r + q] * BS, BS), BS), :]
                for q in range(KB)
            ]
            t = jnp.dot(w, jnp.concatenate(parts, axis=0), preferred_element_type=F32)
            out[pl.ds(pl.multiple_of(i * rows + rr * BS, BS), BS), :] = t.astype(out.dtype)
        return carry

    lax.fori_loop(0, chunks, body, 0)


def input_grad_part(rows, place, col, w, both, dtype):
    smem = pl.BlockSpec(memory_space=SMEM)
    vmem = pl.BlockSpec(memory_space=VMEM)
    return pl.pallas_call(
        functools.partial(input_grad_kernel, rows),
        in_specs=[smem, smem, vmem, vmem],
        out_specs=vmem,
        out_shape=jax.ShapeDtypeStruct((place.shape[0] * rows, both.shape[1]), dtype),
        compiler_params=pltpu.CompilerParams(vmem_limit_bytes=16 << 20),
        cost_estimate=pl.CostEstimate(flops=1 << 29, bytes_accessed=4 << 20, transcendentals=0),
        name="input_grad_part",
    )(place, col, w, both)


def grads_kernel(groups, pieces, capacity, batch, is_up, *refs):
    tab, order, place = refs[:3]
    feature_refs = refs[3 : 3 + groups * pieces]
    both_refs = refs[3 + groups * pieces : 3 + groups * pieces + groups]
    out = refs[3 + groups * pieces + groups]
    features, tiles, sem = refs[4 + groups * pieces + groups :]
    size = feature_refs[0].shape[0]
    base = both_refs[0].shape[0] // 2 if is_up else 0
    copies = []
    for g in range(groups):
        for p in range(pieces):
            n = g * pieces + p
            copies.append(
                pltpu.make_async_copy(
                    feature_refs[n], features.at[g, pl.ds(p * size, size), :], sem.at[n]
                )
            )
    for copy in copies:
        copy.start()
    for copy in copies:
        copy.wait()
    low = lax.broadcasted_iota(jnp.int32, (batch, 2 * BS), 1) < BS

    def body(b, carry):
        for u in range(batch):
            e = tab[b * batch + u]
            live = e >= 0
            e = jnp.maximum(e, 0)
            at = pl.multiple_of(place[e // KB], BS)
            to = pl.multiple_of(base + order[e] * BS, BS)
            f = jnp.concatenate([features[g, pl.ds(at, BS), :] for g in range(groups)], axis=1)
            h = jnp.concatenate([ref[pl.ds(to, BS), :] for ref in both_refs], axis=1)
            left, right = (f, h) if is_up else (h, f)
            right = jnp.concatenate([right, right], axis=0)
            t = lax.dot_general(
                left, right, (((1,), (1,)), ((), ())), preferred_element_type=F32
            )
            tiles[u * PITCH : u * PITCH + BS, :] = jnp.where(live, t, 0.0)
        for a in range(BS // 2):
            even = tiles[pl.ds(2 * a, batch, stride=PITCH), :]
            odd = tiles[pl.ds(2 * a + 1, batch, stride=PITCH), :]
            out[
                pl.ds(pl.multiple_of(b * batch, batch), batch), a * 2 * BS : (a + 1) * 2 * BS
            ] = jnp.where(low, even, odd).astype(BF)
        return carry

    lax.fori_loop(0, capacity // batch, body, 0)


def owned_grads(tab, order, place, features, boths, capacity, is_up):
    groups = len(boths)
    pieces = len(features[0])
    batch = GROUP if capacity % GROUP == 0 else 8
    flat = [piece for group in features for piece in group]
    tokens = boths[0].shape[1]
    total = sum(piece.shape[0] for piece in features[0])
    smem = pl.BlockSpec(memory_space=SMEM)
    vmem = pl.BlockSpec(memory_space=VMEM)
    return pl.pallas_call(
        functools.partial(grads_kernel, groups, pieces, capacity, batch, is_up),
        in_specs=[smem] * 3 + [pl.BlockSpec(memory_space=ANY)] * len(flat) + [vmem] * groups,
        out_specs=vmem,
        out_shape=jax.ShapeDtypeStruct((capacity, BS * BS), BF),
        scratch_shapes=[
            VMEM((groups, total, tokens), BF),
            VMEM((batch * PITCH, 2 * BS), F32),
            pltpu.SemaphoreType.DMA((groups * pieces,)),
        ],
        compiler_params=pltpu.CompilerParams(vmem_limit_bytes=48 << 20),
        cost_estimate=pl.CostEstimate(
            flops=2 * capacity * BS * BS * tokens * groups * 4,
            bytes_accessed=6 << 20,
            transcendentals=0,
        ),
        name="grads_up" if is_up else "grads_down",
    )(tab, order, place, *flat, *boths)


def per_device(inputs, cotangent, w_up, w_down, col_up, row_down, owner_up, owner_down):
    rows, tokens = inputs.shape
    blocks = w_up.shape[0]
    groups = lax.axis_size("dp")
    members = lax.axis_size("mp")
    capacity = 5 * blocks // (4 * groups)
    ff = FBLK * BS
    me = lax.axis_index("mp")
    far = members // 4
    half = members // 2

    step = jnp.arange(half, dtype=jnp.int32)
    masks = (step // far) * 2 + (step % far) * 4
    mine = jnp.bitwise_xor(me, masks).astype(jnp.int32)
    other = jnp.bitwise_xor(mine, 1)
    near_place = jnp.concatenate([mine[:far], other[:far]])
    after = lax.optimization_barrier

    others = range(1, groups)
    in_parts = [inputs] + [swap(inputs, "mp", 4 * z) for z in range(1, far)]
    up_w, down_w = relayout(w_up, w_down)
    in_parts, up_w, down_w = after((in_parts, up_w, down_w))
    in_near = jnp.concatenate(in_parts, axis=0)
    in_far = swap(in_near, "mp", 2)
    in_near_o = [swap(in_near, "dp", d) for d in others]
    in_near_b = swap(in_near, "mp", 1)
    in_near, cotangent = after((in_near, cotangent))
    cot_parts = [cotangent] + [swap(cotangent, "mp", 4 * z) for z in range(1, far)]
    up_tab, down_tab = slots(
        lax.axis_index("dp").reshape(1), owner_up[:, 0], owner_down[:, 0]
    )
    hidden = hidden_sum(rows, True, near_place, col_up, up_w, [in_near, in_near_b])
    cot_parts, hidden, up_tab, down_tab = after((cot_parts, hidden, up_tab, down_tab))
    cot_near = jnp.concatenate(cot_parts, axis=0)
    cot_far = swap(cot_near, "mp", 2)
    in_far_o = [swap(in_far, "dp", d) for d in others]
    in_far_b = swap(in_far, "mp", 1)
    cot_near_b = swap(cot_near, "mp", 1)
    cot_near_o = [swap(cot_near, "dp", d) for d in others]
    hidden = hidden_sum(
        rows, True, jnp.concatenate([mine[far:], other[far:]]), col_up, up_w,
        [in_far, in_far_b], hidden,
    )
    upper = hidden_sum(rows, False, near_place, row_down, down_w, [cot_near, cot_near_b])
    cot_far, hidden, upper, in_near_o = after((cot_far, hidden, upper, in_near_o))
    cot_far_b = swap(cot_far, "mp", 1)
    cot_far_o = [swap(cot_far, "dp", d) for d in others]
    upper = hidden_sum(rows, False, mine[far:], row_down, down_w, [cot_far], upper)
    cot_far_b, in_far_o = after((cot_far_b, in_far_o))
    both = hidden_sum(rows, False, other[far:], row_down, down_w, [cot_far_b], upper, hidden)
    both_o = [swap(both, "dp", d) for d in others]

    sent = input_grad_part(rows, other, col_up, up_w, both, BF)
    arrived = swap(sent, "mp", 1)
    terms = input_grad_part(rows, mine, col_up, up_w, both, F32)
    terms = terms + arrived.astype(F32)
    cut = far * rows
    arrived = swap(terms[cut:].astype(BF), "mp", 2)
    arrived, cot_near_o = after((arrived, cot_near_o))
    terms = terms[:cut] + arrived.astype(F32)
    total = terms[:rows]
    pieces = [
        swap(terms[z * rows : (z + 1) * rows].astype(BF), "mp", 4 * z) for z in range(1, far)
    ]

    in_all = [[in_near, in_far, in_near_b, in_far_b]]
    cot_all = [[cot_near, cot_far, cot_near_b, cot_far_b]]
    both_all = [both] + both_o
    for d in others:
        ours = [in_near_o[d - 1], in_far_o[d - 1]]
        in_all.append(ours + [swap(x, "mp", 1) for x in ours])
        ours = [cot_near_o[d - 1], cot_far_o[d - 1]]
        cot_all.append(ours + [swap(x, "mp", 1) for x in ours])

    row = jnp.arange(members * rows // BS, dtype=jnp.int32)
    apart = jnp.bitwise_xor(row // (rows // BS), me)
    spot = (apart & 1) * half + ((apart >> 1) & 1) * far + (apart >> 2)
    place = spot * rows + (row % (rows // BS)) * BS
    grad_up = owned_grads(up_tab, col_up, place, in_all, both_all, capacity, True)
    pieces, grad_up = after((pieces, grad_up))
    for piece in pieces:
        total = total + piece.astype(F32)
    input_grad = total.astype(BF)
    grad_down = owned_grads(down_tab, row_down, place, cot_all, both_all, capacity, False)
    return both[:ff], input_grad, grad_up, grad_down


def solution(mesh):
    placed = (
        P("mp", "dp"),
        P("mp", "dp"),
        P("mp", None),
        P("mp", None),
        P("mp"),
        P("mp"),
        P("mp", None),
        P("mp", None),
    )
    return jax.shard_map(
        per_device,
        mesh=mesh,
        in_specs=placed,
        out_specs=(P("mp", "dp"), P("mp", "dp"), P(("dp", "mp"), None), P(("dp", "mp"), None)),
        check_vma=False,
    )
```

```python
import functools
import jax
import jax.numpy as jnp
from jax import lax
from jax.experimental import pallas as pl
from jax.experimental.pallas import tpu as pltpu
from jax.sharding import PartitionSpec as P

BS = 64
FBLK = 16
KB = 2
GROUP = 16
RELAYOUT = 64
PITCH = BS + 1
VMEM = pltpu.VMEM
SMEM = pltpu.SMEM
ANY = pl.ANY
BF = jnp.bfloat16
F32 = jnp.float32
COST = pl.CostEstimate(flops=1 << 29, bytes_accessed=6 << 20, transcendentals=0)
SMALL = pl.CostEstimate(flops=1000, bytes_accessed=1 << 20, transcendentals=0)


def swap(value, axis, mask):
    size = lax.axis_size(axis)
    return lax.ppermute(value, axis, [(i, i ^ mask) for i in range(size)])


def swap_groups(value, group_mask, mask):
    groups, size = lax.axis_size("dp"), lax.axis_size("mp")
    pairs = [
        (g * size + i, (g ^ group_mask) * size + (i ^ mask))
        for g in range(groups)
        for i in range(size)
    ]
    return lax.ppermute(value, ("dp", "mp"), pairs)


def relayout_kernel(blocks, src, out, tall):
    lane = lax.broadcasted_iota(jnp.int32, (BS, 2 * BS), 1) < BS
    even = lax.broadcasted_iota(jnp.int32, (blocks, 2 * BS), 0) % 2 == 0

    def body(i, carry):
        rows = pl.ds(pl.multiple_of(i * blocks, blocks), blocks)
        for a in range(BS // 2):
            tile = src[rows, a * 2 * BS : (a + 1) * 2 * BS].astype(F32)
            turned = pltpu.roll(tile, BS, 1)
            tall[pl.ds(2 * a, blocks, stride=PITCH), :] = jnp.where(even, tile, turned)
            tall[pl.ds(2 * a + 1, blocks, stride=PITCH), :] = jnp.where(even, turned, tile)
        for r in range(blocks // KB):
            first = tall[2 * r * PITCH : 2 * r * PITCH + BS, :]
            second = tall[(2 * r + 1) * PITCH : (2 * r + 1) * PITCH + BS, :]
            at = pl.multiple_of(i * (blocks // KB) * BS + r * BS, BS)
            out[pl.ds(at, BS), :] = jnp.where(lane, first, second).astype(BF)
        return carry

    lax.fori_loop(0, src.shape[0] // blocks, body, 0)


def relayout(w):
    vmem = pl.BlockSpec(memory_space=VMEM)
    return pl.pallas_call(
        functools.partial(relayout_kernel, RELAYOUT),
        in_specs=[vmem],
        out_specs=vmem,
        out_shape=jax.ShapeDtypeStruct((w.shape[0] * BS // KB, KB * BS), BF),
        scratch_shapes=[VMEM((RELAYOUT * PITCH, 2 * BS), F32)],
        compiler_params=pltpu.CompilerParams(vmem_limit_bytes=16 << 20),
        cost_estimate=COST,
        name="relayout",
    )(w)


def slots_kernel(me_ref, up_ref, down_ref, up_tab, down_tab, counts):
    group = me_ref[0]
    total = up_ref.shape[0]

    def body(i, carry):
        a, b = carry
        for u in range(8):
            e = i * 8 + u
            up_tab[a] = e
            down_tab[b] = e
            a = a + (up_ref[e] == group).astype(jnp.int32)
            b = b + (down_ref[e] == group).astype(jnp.int32)
        return a, b

    a, b = lax.fori_loop(0, total // 8, body, (jnp.int32(0), jnp.int32(0)))
    counts[0] = a
    counts[1] = b


def slots(group, owner_up, owner_down):
    total = owner_up.shape[0]
    shape = jax.ShapeDtypeStruct((total + 8,), jnp.int32)
    spec = pl.BlockSpec(memory_space=SMEM)
    return pl.pallas_call(
        slots_kernel,
        in_specs=[spec] * 3,
        out_specs=[spec] * 3,
        out_shape=[shape, shape, jax.ShapeDtypeStruct((2,), jnp.int32)],
        cost_estimate=COST,
        name="slots",
    )(group, owner_up, owner_down)


def gelu_slope(value):
    scale = 0.7978845608028654
    cubic = 0.044715
    inner = scale * (value + cubic * value * value * value)
    tanh_part = jnp.tanh(inner)
    gate = 0.5 * (1.0 + tanh_part)
    slope = gate + 0.5 * value * (1.0 - tanh_part * tanh_part) * scale * (
        1.0 + 3.0 * cubic * value * value
    )
    return value * gate, slope


def source(me, i, far):
    return me ^ ((i // far) * 2 + (i % far) * 4)


def add_blocks(me_ref, where_ref, w_ref, x_refs, starts, acc, rows, is_up):
    far = w_ref.shape[0] // rows // 4
    per = rows // BS
    zero = jnp.zeros((BS, acc.shape[1]), BF)
    width = acc.shape[1]
    for x_ref, (bit, skip) in zip(x_refs, starts):

        def body(i, carry, x_ref=x_ref, bit=bit, skip=skip):
            start = source(me_ref[0] ^ bit, skip + i, far) * per
            for rr in range(per):
                r = start + rr
                w = w_ref[pl.ds(pl.multiple_of(r * BS, BS), BS), :]
                x = x_ref[pl.ds(pl.multiple_of(i * rows + rr * BS, BS), BS), :]
                if is_up:
                    t = lax.dot_general(
                        w, x, (((0,), (0,)), ((), ())), preferred_element_type=F32
                    )
                    parts = [t[q * BS : (q + 1) * BS, :] for q in range(KB)]
                else:
                    right = jnp.concatenate(
                        [
                            jnp.concatenate([x, zero], axis=1),
                            jnp.concatenate([zero, x], axis=1),
                        ],
                        axis=0,
                    )
                    t = jnp.dot(w, right, preferred_element_type=F32)
                    parts = [t[:, q * width : (q + 1) * width] for q in range(KB)]
                for q in range(KB):
                    to = pl.ds(pl.multiple_of(where_ref[KB * r + q] * BS, BS), BS)
                    acc[to, :] += parts[q]
            return carry

        lax.fori_loop(0, x_ref.shape[0] // rows, body, 0)


def hidden_kernel(rows, is_up, starts, first, last, *refs):
    me_ref, where_ref, w_ref = refs[:3]
    x_refs = refs[3 : 3 + len(starts)]
    rest = list(refs[3 + len(starts) :])
    acc_in = None if first else rest.pop(0)
    hidden = rest.pop(0) if last else None
    if last:
        both, active, acc = rest
    else:
        (acc,) = rest
    acc[...] = jnp.zeros_like(acc) if first else acc_in[...]
    add_blocks(me_ref, where_ref, w_ref, x_refs, starts, acc, rows, is_up)
    if last:
        ff = acc.shape[0]

        def body(i, carry):
            at = pl.multiple_of(i * BS, BS)
            value, slope = gelu_slope(hidden[pl.ds(at, BS), :])
            both[pl.ds(at, BS), :] = value.astype(BF)
            active[pl.ds(at, BS), :] = value.astype(BF)
            both[pl.ds(ff + at, BS), :] = (acc[pl.ds(at, BS), :] * slope).astype(BF)
            return carry

        lax.fori_loop(0, ff // BS, body, 0)


def hidden_sum(rows, is_up, me, where, w, pieces, starts, acc=None, hidden=None):
    ff, tokens = FBLK * BS, pieces[0].shape[1]
    smem = pl.BlockSpec(memory_space=SMEM)
    vmem = pl.BlockSpec(memory_space=VMEM)
    more = [x for x in (acc, hidden) if x is not None]
    if hidden is None:
        outs, scratch = [jax.ShapeDtypeStruct((ff, tokens), F32)], []
    else:
        outs = [jax.ShapeDtypeStruct((n * ff, tokens), BF) for n in (2, 1)]
        scratch = [VMEM((ff, tokens), F32)]
    return pl.pallas_call(
        functools.partial(
            hidden_kernel, rows, is_up, tuple(starts), acc is None, hidden is not None
        ),
        in_specs=[smem, smem] + [vmem] * (1 + len(pieces) + len(more)),
        out_specs=[vmem] * len(outs),
        out_shape=outs,
        scratch_shapes=scratch,
        compiler_params=pltpu.CompilerParams(vmem_limit_bytes=12 << 20),
        cost_estimate=COST,
        name=("hidden" if is_up else "upper") + ("" if hidden is None else "_last"),
    )(me, where, w, *pieces, *more)


def input_grad_kernel(rows, bit, me_ref, col_ref, w_ref, both_ref, out):
    per = rows // BS
    chunks = out.shape[0] // rows
    base = both_ref.shape[0] // 2

    def body(i, carry):
        start = source(me_ref[0] ^ bit, i, chunks // 2) * per
        for rr in range(per):
            r = start + rr
            w = w_ref[pl.ds(pl.multiple_of(r * BS, BS), BS), :]
            parts = [
                both_ref[pl.ds(pl.multiple_of(base + col_ref[KB * r + q] * BS, BS), BS), :]
                for q in range(KB)
            ]
            t = jnp.dot(w, jnp.concatenate(parts, axis=0), preferred_element_type=F32)
            out[pl.ds(pl.multiple_of(i * rows + rr * BS, BS), BS), :] = t.astype(out.dtype)
        return carry

    lax.fori_loop(0, chunks, body, 0)


def input_grad_part(rows, bit, me, col, w, both, dtype):
    smem = pl.BlockSpec(memory_space=SMEM)
    vmem = pl.BlockSpec(memory_space=VMEM)
    return pl.pallas_call(
        functools.partial(input_grad_kernel, rows, bit),
        in_specs=[smem, smem, vmem, vmem],
        out_specs=vmem,
        out_shape=jax.ShapeDtypeStruct((w.shape[0] // 2, both.shape[1]), dtype),
        compiler_params=pltpu.CompilerParams(vmem_limit_bytes=10 << 20),
        cost_estimate=COST,
        name="input_grad_part",
    )(me, col, w, both)


def in_vmem(kernel, outs, *args):
    vmem = pl.BlockSpec(memory_space=VMEM)
    return pl.pallas_call(
        kernel,
        in_specs=[vmem] * len(args),
        out_specs=[vmem] * len(outs),
        out_shape=[jax.ShapeDtypeStruct(*x) for x in outs],
        compiler_params=pltpu.CompilerParams(vmem_limit_bytes=10 << 20),
        cost_estimate=SMALL,
        name=kernel.__name__,
    )(*args)


def join(parts):
    def join_parts(*refs):
        row = 0
        for ref in refs[:-1]:
            refs[-1][row : row + ref.shape[0], :] = ref[...]
            row += ref.shape[0]

    shape = (sum(x.shape[0] for x in parts), parts[0].shape[1])
    return in_vmem(join_parts, [(shape, parts[0].dtype)], *parts)[0]


def add_and_split(terms, arrived, keep):
    rows, tokens = terms.shape
    sends = (rows - keep) // min(keep, rows - keep)
    size = (rows - keep) // sends

    def add_stage(terms_ref, arrived_ref, keep_ref, *send_refs):
        keep_ref[...] = terms_ref[:keep, :] + arrived_ref[:keep, :].astype(F32)
        for n, ref in enumerate(send_refs):
            at = pl.ds(keep + n * size, size)
            ref[...] = (terms_ref[at, :] + arrived_ref[at, :].astype(F32)).astype(BF)

    outs = [((keep, tokens), F32)] + [((size, tokens), BF)] * sends
    return in_vmem(add_stage, outs, terms, arrived)


def add_all(terms, arrived):
    def add_last(*refs):
        total = refs[0][...]
        for ref in refs[1:-1]:
            total = total + ref[...].astype(F32)
        refs[-1][...] = total.astype(BF)

    return in_vmem(add_last, [(terms.shape, BF)], terms, *arrived)[0]


def grads_kernel(groups, pieces, capacity, batch, rows, is_up, *refs):
    tab, count, order, me_ref = refs[:4]
    flat = refs[4 : 4 + sum(pieces)]
    both_refs = refs[4 + len(flat) : 4 + len(flat) + groups]
    out, features, tiles, *sem = refs[4 + len(flat) + groups :]
    base = both_refs[0].shape[0] // 2 if is_up else 0
    copies = []
    n = 0
    for g in range(groups):
        row = 0
        for _ in range(pieces[g]):
            size = flat[n].shape[0]
            if sem:
                copies.append(
                    pltpu.make_async_copy(
                        flat[n], features.at[g, pl.ds(row, size), :], sem[0].at[n]
                    )
                )
            else:
                features[g, row : row + size, :] = flat[n][...]
            row += size
            n += 1
    for copy in copies:
        copy.start()
    for copy in copies:
        copy.wait()
    low = lax.broadcasted_iota(jnp.int32, (batch, 2 * BS), 1) < BS
    slot = lax.broadcasted_iota(jnp.int32, (batch, 2 * BS), 0)
    live_slots = count[0 if is_up else 1]

    half = features.shape[1] // rows // 2
    far = half // 2
    per = rows // BS

    def place(row, y_first):
        apart = (row // per) ^ me_ref[0]
        core, y, z = apart & 1, (apart >> 1) & 1, apart >> 2
        spot = core * half + (z * 2 + y if y_first else y * far + z)
        return pl.multiple_of(spot * rows + (row % per) * BS, BS)

    def body(b, carry):
        live = slot + b * batch < live_slots
        for u in range(batch):
            e = jnp.where(b * batch + u < live_slots, tab[b * batch + u], 0)
            at = [place(e // KB, g > 0 and not is_up) for g in range(groups)]
            to = pl.multiple_of(base + order[e] * BS, BS)
            f = jnp.concatenate(
                [features[g, pl.ds(at[g], BS), :] for g in range(groups)], axis=1
            )
            h = jnp.concatenate([ref[pl.ds(to, BS), :] for ref in both_refs], axis=1)
            left, right = (f, h) if is_up else (h, f)
            t = lax.dot_general(
                left, right, (((1,), (1,)), ((), ())), preferred_element_type=F32
            )
            tiles[u * PITCH : u * PITCH + BS, :BS] = t
        for a in range(BS // 2):
            even = tiles[pl.ds(2 * a, batch, stride=PITCH), :]
            odd = pltpu.roll(tiles[pl.ds(2 * a + 1, batch, stride=PITCH), :], BS, 1)
            out[
                pl.ds(pl.multiple_of(b * batch, batch), batch), a * 2 * BS : (a + 1) * 2 * BS
            ] = jnp.where(live, jnp.where(low, even, odd), 0.0).astype(BF)
        return carry

    lax.fori_loop(0, capacity // batch, body, 0)


def owned_grads(tab, count, order, me, features, boths, capacity, rows, is_up):
    groups = len(boths)
    pieces = tuple(len(group) for group in features)
    batch = GROUP if capacity % GROUP == 0 else 8
    flat = [piece for group in features for piece in group]
    tokens = boths[0].shape[1]
    total = sum(piece.shape[0] for piece in features[0])
    small = groups * total * tokens <= 4 << 20
    smem = pl.BlockSpec(memory_space=SMEM)
    vmem = pl.BlockSpec(memory_space=VMEM)
    piece = vmem if small else pl.BlockSpec(memory_space=ANY)
    scratch = [VMEM((groups, total, tokens), BF), VMEM((batch * PITCH, 2 * BS), F32)]
    if not small:
        scratch.append(pltpu.SemaphoreType.DMA((len(flat),)))
    return pl.pallas_call(
        functools.partial(grads_kernel, groups, pieces, capacity, batch, rows, is_up),
        in_specs=[smem] * 4 + [piece] * len(flat) + [vmem] * groups,
        out_specs=vmem,
        out_shape=jax.ShapeDtypeStruct((capacity, BS * BS), BF),
        scratch_shapes=scratch,
        compiler_params=pltpu.CompilerParams(vmem_limit_bytes=(20 if small else 48) << 20),
        cost_estimate=COST,
        name="grads_up" if is_up else "grads_down",
    )(tab, count, order, me, *flat, *boths)


def per_device(inputs, cotangent, w_up, w_down, col_up, row_down, owner_up, owner_down):
    rows, tokens = inputs.shape
    blocks = w_up.shape[0]
    groups = lax.axis_size("dp")
    members = lax.axis_size("mp")
    capacity = 5 * blocks // (4 * groups)
    me = lax.axis_index("mp").reshape(1)
    far = members // 4
    half = members // 2
    after = lax.optimization_barrier
    others = range(1, groups)

    cot_x = [swap(cotangent, "dp", d) for d in others]
    cot_xy = [swap_groups(cotangent, d, 2) for d in others]
    in_parts = [inputs] + [swap(inputs, "mp", 4 * z) for z in range(1, far)]
    up_w = relayout(w_up)
    down_w = relayout(w_down)
    in_parts, up_w, down_w, cot_x, cot_xy, cotangent = after(
        (in_parts, up_w, down_w, cot_x, cot_xy, cotangent)
    )
    in_near = join(in_parts)
    in_far = swap(in_near, "mp", 2)
    in_near_o = [swap(in_near, "dp", d) for d in others]
    in_near_b = swap(in_near, "mp", 1)
    cot_parts = [cotangent] + [swap(cotangent, "mp", 4 * z) for z in range(1, far)]
    cot_o = [join([x, xy]) for x, xy in zip(cot_x, cot_xy)]
    (hidden,) = hidden_sum(
        rows, True, me, col_up, up_w, [in_near, in_near_b], [(0, 0), (1, 0)]
    )
    cot_parts, hidden, cot_o, in_far, in_near_o = after(
        (cot_parts, hidden, cot_o, in_far, in_near_o)
    )
    cot_near = join(cot_parts)
    cot_far = swap(cot_near, "mp", 2)
    cot_near_b = swap(cot_near, "mp", 1)
    in_far_b = swap(in_far, "mp", 1)
    in_far_o = [swap(in_far, "dp", d) for d in others]
    cot_o_z = [[swap(x, "mp", 4 * z) for z in range(1, far)] for x in cot_o]
    (upper,) = hidden_sum(
        rows, False, me, row_down, down_w, [cot_near, cot_near_b], [(0, 0), (1, 0)]
    )
    (hidden,) = hidden_sum(
        rows, True, me, col_up, up_w, [in_far, in_far_b], [(0, far), (1, far)], hidden
    )
    early = [x[: far // 2] for x in cot_o_z]
    cot_far, hidden, upper, in_far_o, early = after((cot_far, hidden, upper, in_far_o, early))
    cot_far_b = swap(cot_far, "mp", 1)
    (upper,) = hidden_sum(rows, False, me, row_down, down_w, [cot_far], [(0, far)], upper)
    both, active = hidden_sum(
        rows, False, me, row_down, down_w, [cot_far_b], [(1, far)], upper, hidden
    )
    both_o = [swap(both, "dp", d) for d in others]

    sent = input_grad_part(rows, 1, me, col_up, up_w, both, BF)
    arrived = swap(sent, "mp", 1)
    sent, both = after((sent, both))
    terms = input_grad_part(rows, 0, me, col_up, up_w, both, F32)
    terms, sent = add_and_split(terms, arrived, far * rows)
    arrived = swap(sent, "mp", 2)
    terms, owner_up, owner_down = after((terms, owner_up, owner_down))
    up_tab, down_tab, counts = slots(
        lax.axis_index("dp").reshape(1), owner_up[:, 0], owner_down[:, 0]
    )
    in_near_o_b = [swap(x, "mp", 1) for x in in_near_o]
    in_far_o_b = [swap(x, "mp", 1) for x in in_far_o]
    in_all = [[in_near, in_far, in_near_b, in_far_b]]
    in_all += [list(x) for x in zip(in_near_o, in_far_o, in_near_o_b, in_far_o_b)]
    both_all = [both] + both_o
    grad_up = owned_grads(up_tab, counts, col_up, me, in_all, both_all, capacity, rows, True)
    late = [x[far // 2 :] for x in cot_o_z]
    arrived, late, grad_up = after((arrived, late, grad_up))
    cot_o = [[x] + near + rest for x, near, rest in zip(cot_o, early, late)]
    terms, *sent = add_and_split(terms, arrived, rows)
    pieces = [swap(x, "mp", 4 * z + 4) for z, x in enumerate(sent)]
    cot_o_b = [[swap(piece, "mp", 1) for piece in x] for x in cot_o]
    cot_all = [[cot_near, cot_far, cot_near_b, cot_far_b]]
    cot_all += [x + x_b for x, x_b in zip(cot_o, cot_o_b)]
    grad_down = owned_grads(
        down_tab, counts, row_down, me, cot_all, both_all, capacity, rows, False
    )
    pieces, grad_down = after((pieces, grad_down))
    return active, add_all(terms, pieces), grad_up, grad_down


def solution(mesh):
    placed = (
        P("mp", "dp"),
        P("mp", "dp"),
        P("mp", None),
        P("mp", None),
        P("mp"),
        P("mp"),
        P("mp", None),
        P("mp", None),
    )
    return jax.shard_map(
        per_device,
        mesh=mesh,
        in_specs=placed,
        out_specs=(P("mp", "dp"), P("mp", "dp"), P(("dp", "mp"), None), P(("dp", "mp"), None)),
        check_vma=False,
    )
```

```python
import functools
import jax
import jax.numpy as jnp
from jax import lax
from jax.experimental import pallas as pl
from jax.experimental.pallas import tpu as pltpu
from jax.sharding import PartitionSpec as P

BS = 64
FBLK = 16
KB = 2
GROUP = 16
RELAYOUT = 64
PITCH = BS + 1
VMEM = pltpu.VMEM
SMEM = pltpu.SMEM
ANY = pl.ANY
BF = jnp.bfloat16
F32 = jnp.float32
COST = pl.CostEstimate(flops=1 << 29, bytes_accessed=6 << 20, transcendentals=0)
SMALL = pl.CostEstimate(flops=1000, bytes_accessed=1 << 20, transcendentals=0)


def swap(value, axis, mask):
    size = lax.axis_size(axis)
    return lax.ppermute(value, axis, [(i, i ^ mask) for i in range(size)])


def swap_groups(value, group_mask, mask):
    groups, size = lax.axis_size("dp"), lax.axis_size("mp")
    pairs = [
        (g * size + i, (g ^ group_mask) * size + (i ^ mask))
        for g in range(groups)
        for i in range(size)
    ]
    return lax.ppermute(value, ("dp", "mp"), pairs)


def relayout_kernel(blocks, src, out, tall):
    lane = lax.broadcasted_iota(jnp.int32, (BS, 2 * BS), 1) < BS
    even = lax.broadcasted_iota(jnp.int32, (blocks, 2 * BS), 0) % 2 == 0

    def body(i, carry):
        rows = pl.ds(pl.multiple_of(i * blocks, blocks), blocks)
        for a in range(BS // 2):
            tile = src[rows, a * 2 * BS : (a + 1) * 2 * BS].astype(F32)
            turned = pltpu.roll(tile, BS, 1)
            tall[pl.ds(2 * a, blocks, stride=PITCH), :] = jnp.where(even, tile, turned)
            tall[pl.ds(2 * a + 1, blocks, stride=PITCH), :] = jnp.where(even, turned, tile)
        for r in range(blocks // KB):
            first = tall[2 * r * PITCH : 2 * r * PITCH + BS, :]
            second = tall[(2 * r + 1) * PITCH : (2 * r + 1) * PITCH + BS, :]
            at = pl.multiple_of(i * (blocks // KB) * BS + r * BS, BS)
            out[pl.ds(at, BS), :] = jnp.where(lane, first, second).astype(BF)
        return carry

    lax.fori_loop(0, src.shape[0] // blocks, body, 0)


def relayout(w):
    vmem = pl.BlockSpec(memory_space=VMEM)
    return pl.pallas_call(
        functools.partial(relayout_kernel, RELAYOUT),
        in_specs=[vmem],
        out_specs=vmem,
        out_shape=jax.ShapeDtypeStruct((w.shape[0] * BS // KB, KB * BS), BF),
        scratch_shapes=[VMEM((RELAYOUT * PITCH, 2 * BS), F32)],
        compiler_params=pltpu.CompilerParams(vmem_limit_bytes=16 << 20),
        cost_estimate=COST,
        name="relayout",
    )(w)


def slots_kernel(me_ref, up_ref, down_ref, up_tab, down_tab, counts):
    group = me_ref[0]
    total = up_ref.shape[0]

    def body(i, carry):
        a, b = carry
        for u in range(8):
            e = i * 8 + u
            up_tab[a] = e
            down_tab[b] = e
            a = a + (up_ref[e] == group).astype(jnp.int32)
            b = b + (down_ref[e] == group).astype(jnp.int32)
        return a, b

    a, b = lax.fori_loop(0, total // 8, body, (jnp.int32(0), jnp.int32(0)))
    counts[0] = a
    counts[1] = b


def slots(group, owner_up, owner_down):
    total = owner_up.shape[0]
    shape = jax.ShapeDtypeStruct((total + 8,), jnp.int32)
    spec = pl.BlockSpec(memory_space=SMEM)
    return pl.pallas_call(
        slots_kernel,
        in_specs=[spec] * 3,
        out_specs=[spec] * 3,
        out_shape=[shape, shape, jax.ShapeDtypeStruct((2,), jnp.int32)],
        cost_estimate=COST,
        name="slots",
    )(group, owner_up, owner_down)


def gelu_slope(value):
    scale = 0.7978845608028654
    cubic = 0.044715
    inner = scale * (value + cubic * value * value * value)
    tanh_part = jnp.tanh(inner)
    gate = 0.5 * (1.0 + tanh_part)
    slope = gate + 0.5 * value * (1.0 - tanh_part * tanh_part) * scale * (
        1.0 + 3.0 * cubic * value * value
    )
    return value * gate, slope


def source(me, i, far):
    return me ^ ((i // far) * 2 + (i % far) * 4)


def add_blocks(me_ref, where_ref, w_ref, x_refs, starts, acc, rows, is_up):
    far = w_ref.shape[0] // rows // 4
    per = rows // BS
    zero = jnp.zeros((BS, acc.shape[1]), BF)
    width = acc.shape[1]
    for x_ref, (bit, skip) in zip(x_refs, starts):

        def body(i, carry, x_ref=x_ref, bit=bit, skip=skip):
            start = source(me_ref[0] ^ bit, skip + i, far) * per
            for rr in range(per):
                r = start + rr
                w = w_ref[pl.ds(pl.multiple_of(r * BS, BS), BS), :]
                x = x_ref[pl.ds(pl.multiple_of(i * rows + rr * BS, BS), BS), :]
                if is_up:
                    t = lax.dot_general(
                        w, x, (((0,), (0,)), ((), ())), preferred_element_type=F32
                    )
                    parts = [t[q * BS : (q + 1) * BS, :] for q in range(KB)]
                else:
                    right = jnp.concatenate(
                        [
                            jnp.concatenate([x, zero], axis=1),
                            jnp.concatenate([zero, x], axis=1),
                        ],
                        axis=0,
                    )
                    t = jnp.dot(w, right, preferred_element_type=F32)
                    parts = [t[:, q * width : (q + 1) * width] for q in range(KB)]
                for q in range(KB):
                    to = pl.ds(pl.multiple_of(where_ref[KB * r + q] * BS, BS), BS)
                    acc[to, :] += parts[q]
            return carry

        lax.fori_loop(0, x_ref.shape[0] // rows, body, 0)


def hidden_kernel(rows, is_up, starts, first, last, *refs):
    me_ref, where_ref, w_ref = refs[:3]
    x_refs = refs[3 : 3 + len(starts)]
    rest = list(refs[3 + len(starts) :])
    acc_in = None if first else rest.pop(0)
    if not last:
        (acc,) = rest
    elif is_up:
        active, slope_ref, acc = rest
    else:
        slope_ref, slope_grad, acc = rest
    acc[...] = jnp.zeros_like(acc) if first else acc_in[...]
    add_blocks(me_ref, where_ref, w_ref, x_refs, starts, acc, rows, is_up)
    if last:
        ff = acc.shape[0]

        def body(i, carry):
            here = pl.ds(pl.multiple_of(i * BS, BS), BS)
            if is_up:
                value, slope = gelu_slope(acc[here, :])
                active[here, :] = value.astype(BF)
                slope_ref[here, :] = slope
            else:
                slope_grad[here, :] = (acc[here, :] * slope_ref[here, :]).astype(BF)
            return carry

        lax.fori_loop(0, ff // BS, body, 0)


def hidden_sum(rows, is_up, me, where, w, pieces, starts, acc=None, last=False, slope=None):
    ff, tokens = FBLK * BS, pieces[0].shape[1]
    smem = pl.BlockSpec(memory_space=SMEM)
    vmem = pl.BlockSpec(memory_space=VMEM)
    more = [x for x in (acc, slope) if x is not None]
    whole, kept = jax.ShapeDtypeStruct((ff, tokens), F32), jax.ShapeDtypeStruct((ff, tokens), BF)
    if not last:
        outs = [whole]
    elif is_up:
        outs = [kept, whole]
    else:
        outs = [kept]
    return pl.pallas_call(
        functools.partial(hidden_kernel, rows, is_up, tuple(starts), acc is None, last),
        in_specs=[smem, smem] + [vmem] * (1 + len(pieces) + len(more)),
        out_specs=[vmem] * len(outs),
        out_shape=outs,
        scratch_shapes=[VMEM((ff, tokens), F32)] if last else [],
        compiler_params=pltpu.CompilerParams(vmem_limit_bytes=12 << 20),
        cost_estimate=COST,
        name=("hidden" if is_up else "upper") + ("_last" if last else ""),
    )(me, where, w, *pieces, *more)


def input_grad_kernel(rows, skip, bits, me_ref, col_ref, w_ref, s_ref, *outs):
    per = rows // BS
    chunks = outs[0].shape[0] // rows

    def one(i, bit, out):
        start = source(me_ref[0] ^ bit, skip + i, chunks) * per
        for rr in range(per):
            r = start + rr
            w = w_ref[pl.ds(pl.multiple_of(r * BS, BS), BS), :]
            parts = [
                s_ref[pl.ds(pl.multiple_of(col_ref[KB * r + q] * BS, BS), BS), :]
                for q in range(KB)
            ]
            t = jnp.dot(w, jnp.concatenate(parts, axis=0), preferred_element_type=F32)
            out[pl.ds(pl.multiple_of(i * rows + rr * BS, BS), BS), :] = t.astype(out.dtype)

    def body(i, carry):
        for bit, out in zip(bits, outs):
            one(i, bit, out)
        return carry

    lax.fori_loop(0, chunks, body, 0)


def input_grad_part(rows, skip, bits, me, col, w, slope_grad):
    smem = pl.BlockSpec(memory_space=SMEM)
    vmem = pl.BlockSpec(memory_space=VMEM)
    shape = (w.shape[0] // 4, slope_grad.shape[1])
    return pl.pallas_call(
        functools.partial(input_grad_kernel, rows, skip, bits),
        in_specs=[smem, smem, vmem, vmem],
        out_specs=[vmem] * len(bits),
        out_shape=[jax.ShapeDtypeStruct(shape, BF if bit else F32) for bit in bits],
        compiler_params=pltpu.CompilerParams(vmem_limit_bytes=10 << 20),
        cost_estimate=COST,
        name="input_grad_part",
    )(me, col, w, slope_grad)


def in_vmem(kernel, outs, *args):
    vmem = pl.BlockSpec(memory_space=VMEM)
    return pl.pallas_call(
        kernel,
        in_specs=[vmem] * len(args),
        out_specs=[vmem] * len(outs),
        out_shape=[jax.ShapeDtypeStruct(*x) for x in outs],
        compiler_params=pltpu.CompilerParams(vmem_limit_bytes=10 << 20),
        cost_estimate=SMALL,
        name=kernel.__name__,
    )(*args)


def join(parts):
    def join_parts(*refs):
        row = 0
        for ref in refs[:-1]:
            refs[-1][row : row + ref.shape[0], :] = ref[...]
            row += ref.shape[0]

    shape = (sum(x.shape[0] for x in parts), parts[0].shape[1])
    return in_vmem(join_parts, [(shape, parts[0].dtype)], *parts)[0]


def add_and_split(terms, arrived, keep):
    rows, tokens = terms.shape
    size = keep if keep else rows
    sends = (rows - keep) // size

    def add_stage(terms_ref, *refs):
        arrived_refs, outs = refs[: len(arrived)], refs[len(arrived) :]
        for n, ref in enumerate(outs):
            at = pl.ds(n * size, size)
            total = terms_ref[at, :]
            for more in arrived_refs:
                total = total + more[at, :].astype(F32)
            ref[...] = total.astype(ref.dtype)

    outs = [((keep, tokens), F32)] if keep else []
    outs += [((size, tokens), BF)] * sends
    return in_vmem(add_stage, outs, terms, *arrived)


def add_all(terms, arrived):
    def add_last(*refs):
        total = refs[0][...]
        for ref in refs[1:-1]:
            total = total + ref[...].astype(F32)
        refs[-1][...] = total.astype(BF)

    return in_vmem(add_last, [(terms.shape, BF)], terms, *arrived)[0]


def grads_kernel(groups, pieces, capacity, batch, rows, is_up, *refs):
    tab, count, order, me_ref = refs[:4]
    flat = refs[4 : 4 + sum(pieces)]
    hidden_refs = refs[4 + len(flat) : 4 + len(flat) + groups]
    out, features, tiles_a, tiles_b, *sem = refs[4 + len(flat) + groups :]
    copies = []
    n = 0
    for g in range(groups):
        row = 0
        for _ in range(pieces[g]):
            size = flat[n].shape[0]
            if sem:
                copies.append(
                    pltpu.make_async_copy(
                        flat[n], features.at[g, pl.ds(row, size), :], sem[0].at[n]
                    )
                )
            else:
                features[g, row : row + size, :] = flat[n][...]
            row += size
            n += 1
    for copy in copies:
        copy.start()
    for copy in copies:
        copy.wait()
    low = lax.broadcasted_iota(jnp.int32, (batch, 2 * BS), 1) < BS
    slot = lax.broadcasted_iota(jnp.int32, (batch, 2 * BS), 0)
    live_slots = count[0 if is_up else 1]

    half = features.shape[1] // rows // 2
    far_bits = (half // 2).bit_length() - 1
    per = rows // BS
    per_bits = per.bit_length() - 1

    def place(row, y_first):
        apart = lax.shift_right_logical(row, per_bits) ^ me_ref[0]
        core, y = apart & 1, lax.shift_right_logical(apart, 1) & 1
        z = lax.shift_right_logical(apart, 2)
        spot = core * half + (z * 2 + y if y_first else (y << far_bits) + z)
        return pl.multiple_of(spot * rows + (row & (per - 1)) * BS, BS)

    def multiply(first, tiles):
        for u in range(batch):
            e = jnp.where(first + u < live_slots, tab[first + u], 0)
            row = lax.shift_right_logical(e, KB.bit_length() - 1)
            at = [place(row, False)]
            at += [at[0] if is_up else place(row, True)] * (groups - 1)
            to = pl.multiple_of(order[e] * BS, BS)
            f = jnp.concatenate(
                [features[g, pl.ds(at[g], BS), :] for g in range(groups)], axis=1
            )
            h = jnp.concatenate([ref[pl.ds(to, BS), :] for ref in hidden_refs], axis=1)
            left, right = (f, h) if is_up else (h, f)
            t = lax.dot_general(
                left, right, (((1,), (1,)), ((), ())), preferred_element_type=F32
            )
            tiles[u * PITCH : u * PITCH + BS, :BS] = t

    def flush(first, tiles):
        live = slot + first < live_slots
        for a in range(BS // 2):
            even = tiles[pl.ds(2 * a, batch, stride=PITCH), :]
            odd = pltpu.roll(tiles[pl.ds(2 * a + 1, batch, stride=PITCH), :], BS, 1)
            out[
                pl.ds(pl.multiple_of(first, batch), batch), a * 2 * BS : (a + 1) * 2 * BS
            ] = jnp.where(live, jnp.where(low, even, odd), 0.0).astype(BF)

    steps = capacity // batch

    def body(i, carry):
        first = i * 2 * batch
        multiply(first, tiles_a)
        multiply(first + batch, tiles_b)
        flush(first, tiles_a)
        flush(first + batch, tiles_b)
        return carry

    lax.fori_loop(0, steps // 2, body, 0)
    if steps % 2:
        multiply(capacity - batch, tiles_a)
        flush(capacity - batch, tiles_a)


def owned_grads(tab, count, order, me, features, hiddens, capacity, rows, is_up):
    groups = len(hiddens)
    pieces = tuple(len(group) for group in features)
    batch = GROUP if capacity % GROUP == 0 else 8
    flat = [piece for group in features for piece in group]
    tokens = hiddens[0].shape[1]
    total = sum(piece.shape[0] for piece in features[0])
    small = groups * total * tokens <= 4 << 20
    smem = pl.BlockSpec(memory_space=SMEM)
    vmem = pl.BlockSpec(memory_space=VMEM)
    piece = vmem if small else pl.BlockSpec(memory_space=ANY)
    scratch = [VMEM((groups, total, tokens), BF)] + [VMEM((batch * PITCH, 2 * BS), F32)] * 2
    if not small:
        scratch.append(pltpu.SemaphoreType.DMA((len(flat),)))
    return pl.pallas_call(
        functools.partial(grads_kernel, groups, pieces, capacity, batch, rows, is_up),
        in_specs=[smem] * 4 + [piece] * len(flat) + [vmem] * groups,
        out_specs=vmem,
        out_shape=jax.ShapeDtypeStruct((capacity, BS * BS), BF),
        scratch_shapes=scratch,
        compiler_params=pltpu.CompilerParams(vmem_limit_bytes=(20 if small else 48) << 20),
        cost_estimate=COST,
        name="grads_up" if is_up else "grads_down",
    )(tab, count, order, me, *flat, *hiddens)


def per_device(inputs, cotangent, w_up, w_down, col_up, row_down, owner_up, owner_down):
    rows, tokens = inputs.shape
    blocks = w_up.shape[0]
    groups = lax.axis_size("dp")
    members = lax.axis_size("mp")
    capacity = 5 * blocks // (4 * groups)
    me = lax.axis_index("mp").reshape(1)
    far = members // 4
    after = lax.optimization_barrier
    others = range(1, groups)

    cot_x = [swap(cotangent, "dp", d) for d in others]
    cot_xy = [swap_groups(cotangent, d, 2) for d in others]
    in_parts = [inputs] + [swap(inputs, "mp", 4 * z) for z in range(1, far)]
    up_w = relayout(w_up)
    cot_parts = [cotangent, swap(cotangent, "mp", 4)]
    in_parts, up_w, cot_x, cot_xy, cot_parts, cotangent = after(
        (in_parts, up_w, cot_x, cot_xy, cot_parts, cotangent)
    )
    in_near = join(in_parts)
    in_far = swap(in_near, "mp", 2)
    in_near_o = [swap(in_near, "dp", d) for d in others]
    in_near_b = swap(in_near, "mp", 1)
    cot_parts += [swap(cotangent, "mp", 4 * z) for z in range(2, far)]
    cot_o = [join([x, xy]) for x, xy in zip(cot_x, cot_xy)]
    in_near_b, cot_o = after((in_near_b, cot_o))
    cot_o_1 = [swap(x, "mp", 4) for x in cot_o]
    (hidden,) = hidden_sum(
        rows, True, me, col_up, up_w, [in_near, in_near_b], [(0, 0), (1, 0)]
    )
    hidden, w_down, owner_up, owner_down = after((hidden, w_down, owner_up, owner_down))
    down_w = relayout(w_down)
    up_tab, down_tab, counts = slots(
        lax.axis_index("dp").reshape(1), owner_up[:, 0], owner_down[:, 0]
    )
    cot_o, cot_o_1, in_near_o, cot_parts, in_far, hidden, down_w, up_tab = after(
        (cot_o, cot_o_1, in_near_o, cot_parts, in_far, hidden, down_w, up_tab)
    )
    cot_near = join(cot_parts)
    cot_far = swap(cot_near, "mp", 2)
    cot_near_b = swap(cot_near, "mp", 1)
    in_far_b = swap(in_far, "mp", 1)
    in_far_o = [swap(in_far, "dp", d) for d in others]
    cot_o_z = [[swap(x, "mp", 4 * z) for z in range(2, far)] for x in cot_o]
    (upper,) = hidden_sum(
        rows, False, me, row_down, down_w, [cot_near, cot_near_b], [(0, 0), (1, 0)]
    )
    active, slope = hidden_sum(
        rows, True, me, col_up, up_w, [in_far, in_far_b], [(0, far), (1, far)], hidden, True
    )
    early = [x[: far // 2 - 1] for x in cot_o_z]
    cot_far, slope, upper, in_far_o, early = after((cot_far, slope, upper, in_far_o, early))
    cot_far_b = swap(cot_far, "mp", 1)
    (upper,) = hidden_sum(rows, False, me, row_down, down_w, [cot_far], [(0, far)], upper)
    (slope_grad,) = hidden_sum(
        rows, False, me, row_down, down_w, [cot_far_b], [(1, far)], upper, True,
        slope,
    )
    slope_grad_o = [swap(slope_grad, "dp", d) for d in others]

    part = functools.partial(input_grad_part, rows)
    (sent,) = part(far, (1,), me, col_up, up_w, slope_grad)
    arrived = swap(sent, "mp", 1)
    (terms,) = part(far, (0,), me, col_up, up_w, slope_grad)
    (sent,) = add_and_split(terms, [arrived], 0)
    arrived = swap(sent, "mp", 2)
    sent, near_slope_grad, near_active = after((sent, slope_grad, active))
    active_o = [swap(near_active, "dp", d) for d in others]
    sent_b, terms = part(0, (1, 0), me, col_up, up_w, near_slope_grad)
    arrived_b = swap(sent_b, "mp", 1)
    in_near_o_b = [swap(x, "mp", 1) for x in in_near_o]
    in_far_o_b = [swap(x, "mp", 1) for x in in_far_o]
    in_all = [[in_near, in_far, in_near_b, in_far_b]]
    in_all += [list(x) for x in zip(in_near_o, in_far_o, in_near_o_b, in_far_o_b)]
    late = [x[far // 2 - 1 :] for x in cot_o_z]
    arrived, late, slope_grad_o, terms = after((arrived, late, slope_grad_o, terms))
    cot_o = [
        [x, x_1] + near + rest for x, x_1, near, rest in zip(cot_o, cot_o_1, early, late)
    ]
    terms, *sent = add_and_split(terms, [arrived, arrived_b], rows)
    pieces = [swap(x, "mp", 4 * z + 4) for z, x in enumerate(sent)]
    cot_o_b = [[swap(piece, "mp", 1) for piece in x] for x in cot_o]
    cot_all = [[cot_near, cot_far, cot_near_b, cot_far_b]]
    cot_all += [x + x_b for x, x_b in zip(cot_o, cot_o_b)]
    grad_up = owned_grads(
        up_tab, counts, col_up, me, in_all, [slope_grad] + slope_grad_o, capacity, rows, True
    )
    grad_down = owned_grads(
        down_tab, counts, row_down, me, cot_all, [active] + active_o, capacity, rows, False
    )
    pieces, grad_up, grad_down = after((pieces, grad_up, grad_down))
    return active, add_all(terms, pieces), grad_up, grad_down


def solution(mesh):
    placed = (
        P("mp", "dp"),
        P("mp", "dp"),
        P("mp", None),
        P("mp", None),
        P("mp"),
        P("mp"),
        P("mp", None),
        P("mp", None),
    )
    return jax.shard_map(
        per_device,
        mesh=mesh,
        in_specs=placed,
        out_specs=(P("mp", "dp"), P("mp", "dp"), P(("dp", "mp"), None), P(("dp", "mp"), None)),
        check_vma=False,
    )
```

```python
import functools
import jax
import jax.numpy as jnp
from jax import lax
from jax.experimental import pallas as pl
from jax.experimental.pallas import tpu as pltpu
from jax.sharding import PartitionSpec as P

BS = 64
FBLK = 16
KB = 2
GROUP = 16
RELAYOUT = 64
PITCH = BS + 1
VMEM = pltpu.VMEM
SMEM = pltpu.SMEM
ANY = pl.ANY
BF = jnp.bfloat16
F32 = jnp.float32
COST = pl.CostEstimate(flops=1 << 29, bytes_accessed=6 << 20, transcendentals=0)
SMALL = pl.CostEstimate(flops=1000, bytes_accessed=1 << 20, transcendentals=0)


def swap(value, axis, mask):
    size = lax.axis_size(axis)
    return lax.ppermute(value, axis, [(i, i ^ mask) for i in range(size)])


def swap_groups(value, group_mask, mask):
    groups, size = lax.axis_size("dp"), lax.axis_size("mp")
    pairs = [
        (g * size + i, (g ^ group_mask) * size + (i ^ mask))
        for g in range(groups)
        for i in range(size)
    ]
    return lax.ppermute(value, ("dp", "mp"), pairs)


def relayout_kernel(blocks, src, out, tall):
    lane = lax.broadcasted_iota(jnp.int32, (BS, 2 * BS), 1) < BS
    even = lax.broadcasted_iota(jnp.int32, (blocks, 2 * BS), 0) % 2 == 0

    def body(i, carry):
        rows = pl.ds(pl.multiple_of(i * blocks, blocks), blocks)
        for a in range(BS // 2):
            tile = src[rows, a * 2 * BS : (a + 1) * 2 * BS].astype(F32)
            turned = pltpu.roll(tile, BS, 1)
            tall[pl.ds(2 * a, blocks, stride=PITCH), :] = jnp.where(even, tile, turned)
            tall[pl.ds(2 * a + 1, blocks, stride=PITCH), :] = jnp.where(even, turned, tile)
        for r in range(blocks // KB):
            first = tall[2 * r * PITCH : 2 * r * PITCH + BS, :]
            second = tall[(2 * r + 1) * PITCH : (2 * r + 1) * PITCH + BS, :]
            at = pl.multiple_of(i * (blocks // KB) * BS + r * BS, BS)
            out[pl.ds(at, BS), :] = jnp.where(lane, first, second).astype(BF)
        return carry

    lax.fori_loop(0, src.shape[0] // blocks, body, 0)


def relayout(w):
    vmem = pl.BlockSpec(memory_space=VMEM)
    return pl.pallas_call(
        functools.partial(relayout_kernel, RELAYOUT),
        in_specs=[vmem],
        out_specs=vmem,
        out_shape=jax.ShapeDtypeStruct((w.shape[0] * BS // KB, KB * BS), BF),
        scratch_shapes=[VMEM((RELAYOUT * PITCH, 2 * BS), F32)],
        compiler_params=pltpu.CompilerParams(vmem_limit_bytes=16 << 20),
        cost_estimate=COST,
        name="relayout",
    )(w)


def slots_kernel(me_ref, up_ref, down_ref, up_tab, down_tab, counts):
    group = me_ref[0]
    total = up_ref.shape[0]

    def body(i, carry):
        a, b = carry
        for u in range(8):
            e = i * 8 + u
            up_tab[a] = e
            down_tab[b] = e
            a = a + (up_ref[e] == group).astype(jnp.int32)
            b = b + (down_ref[e] == group).astype(jnp.int32)
        return a, b

    a, b = lax.fori_loop(0, total // 8, body, (jnp.int32(0), jnp.int32(0)))
    counts[0] = a
    counts[1] = b


def slots(group, owner_up, owner_down):
    total = owner_up.shape[0]
    shape = jax.ShapeDtypeStruct((total + 8,), jnp.int32)
    spec = pl.BlockSpec(memory_space=SMEM)
    return pl.pallas_call(
        slots_kernel,
        in_specs=[spec] * 3,
        out_specs=[spec] * 3,
        out_shape=[shape, shape, jax.ShapeDtypeStruct((2,), jnp.int32)],
        cost_estimate=COST,
        name="slots",
    )(group, owner_up, owner_down)


def gelu_slope(value):
    scale = 0.7978845608028654
    cubic = 0.044715
    inner = scale * (value + cubic * value * value * value)
    tanh_part = jnp.tanh(inner)
    gate = 0.5 * (1.0 + tanh_part)
    slope = gate + 0.5 * value * (1.0 - tanh_part * tanh_part) * scale * (
        1.0 + 3.0 * cubic * value * value
    )
    return value * gate, slope


def source(me, i, far):
    return me ^ ((i // far) * 2 + (i % far) * 4)


def add_blocks(me_ref, where_ref, w_ref, x_refs, starts, acc, rows, is_up):
    far = w_ref.shape[0] // rows // 4
    per = rows // BS
    zero = jnp.zeros((BS, acc.shape[1]), BF)
    width = acc.shape[1]
    for x_ref, (bit, skip) in zip(x_refs, starts):

        def body(i, carry, x_ref=x_ref, bit=bit, skip=skip):
            start = source(me_ref[0] ^ bit, skip + i, far) * per
            for rr in range(per):
                r = start + rr
                w = w_ref[pl.ds(pl.multiple_of(r * BS, BS), BS), :]
                x = x_ref[pl.ds(pl.multiple_of(i * rows + rr * BS, BS), BS), :]
                if is_up:
                    t = lax.dot_general(
                        w, x, (((0,), (0,)), ((), ())), preferred_element_type=F32
                    )
                    parts = [t[q * BS : (q + 1) * BS, :] for q in range(KB)]
                else:
                    right = jnp.concatenate(
                        [
                            jnp.concatenate([x, zero], axis=1),
                            jnp.concatenate([zero, x], axis=1),
                        ],
                        axis=0,
                    )
                    t = jnp.dot(w, right, preferred_element_type=F32)
                    parts = [t[:, q * width : (q + 1) * width] for q in range(KB)]
                for q in range(KB):
                    to = pl.ds(pl.multiple_of(where_ref[KB * r + q] * BS, BS), BS)
                    acc[to, :] += parts[q]
            return carry

        lax.fori_loop(0, x_ref.shape[0] // rows, body, 0)


def hidden_kernel(rows, is_up, starts, first, last, *refs):
    me_ref, where_ref, w_ref = refs[:3]
    x_refs = refs[3 : 3 + len(starts)]
    rest = list(refs[3 + len(starts) :])
    acc_in = None if first else rest.pop(0)
    if not last:
        (acc,) = rest
    elif is_up:
        active, slope_ref, acc = rest
    else:
        slope_ref, col_ref, up_ref, slope_grad, sent, acc = rest
    acc[...] = jnp.zeros_like(acc) if first else acc_in[...]
    add_blocks(me_ref, where_ref, w_ref, x_refs, starts, acc, rows, is_up)
    if last:
        ff = acc.shape[0]

        def body(i, carry):
            here = pl.ds(pl.multiple_of(i * BS, BS), BS)
            if is_up:
                value, slope = gelu_slope(acc[here, :])
                active[here, :] = value.astype(BF)
                slope_ref[here, :] = slope
            else:
                slope_grad[here, :] = (acc[here, :] * slope_ref[here, :]).astype(BF)
            return carry

        lax.fori_loop(0, ff // BS, body, 0)
        if not is_up:
            skip = up_ref.shape[0] // rows // 4
            input_grad_kernel(rows, skip, (1,), me_ref, col_ref, up_ref, slope_grad, sent)


def hidden_sum(rows, is_up, me, where, w, pieces, starts, acc=None, last=False, slope=None, up=()):
    ff, tokens = FBLK * BS, pieces[0].shape[1]
    smem = pl.BlockSpec(memory_space=SMEM)
    vmem = pl.BlockSpec(memory_space=VMEM)
    more = [x for x in (acc, slope) if x is not None]
    whole, kept = jax.ShapeDtypeStruct((ff, tokens), F32), jax.ShapeDtypeStruct((ff, tokens), BF)
    if not last:
        outs = [whole]
    elif is_up:
        outs = [kept, whole]
    else:
        outs = [kept, jax.ShapeDtypeStruct((w.shape[0] // 4, tokens), BF)]
    return pl.pallas_call(
        functools.partial(hidden_kernel, rows, is_up, tuple(starts), acc is None, last),
        in_specs=[smem, smem] + [vmem] * (1 + len(pieces) + len(more)) + [smem, vmem][: len(up)],
        out_specs=[vmem] * len(outs),
        out_shape=outs,
        scratch_shapes=[VMEM((ff, tokens), F32)] if last else [],
        compiler_params=pltpu.CompilerParams(vmem_limit_bytes=12 << 20),
        cost_estimate=COST,
        name=("hidden" if is_up else "upper") + ("_last" if last else ""),
    )(me, where, w, *pieces, *more, *up)


def input_grad_kernel(rows, skip, bits, me_ref, col_ref, w_ref, s_ref, *outs):
    per = rows // BS
    chunks = outs[0].shape[0] // rows

    def one(i, bit, out):
        start = source(me_ref[0] ^ bit, skip + i, chunks) * per
        for rr in range(per):
            r = start + rr
            w = w_ref[pl.ds(pl.multiple_of(r * BS, BS), BS), :]
            parts = [
                s_ref[pl.ds(pl.multiple_of(col_ref[KB * r + q] * BS, BS), BS), :]
                for q in range(KB)
            ]
            t = jnp.dot(w, jnp.concatenate(parts, axis=0), preferred_element_type=F32)
            out[pl.ds(pl.multiple_of(i * rows + rr * BS, BS), BS), :] = t.astype(out.dtype)

    def body(i, carry):
        for bit, out in zip(bits, outs):
            one(i, bit, out)
        return carry

    lax.fori_loop(0, chunks, body, 0)


def input_grad_part(rows, skip, bits, me, col, w, slope_grad):
    smem = pl.BlockSpec(memory_space=SMEM)
    vmem = pl.BlockSpec(memory_space=VMEM)
    shape = (w.shape[0] // 4, slope_grad.shape[1])
    return pl.pallas_call(
        functools.partial(input_grad_kernel, rows, skip, bits),
        in_specs=[smem, smem, vmem, vmem],
        out_specs=[vmem] * len(bits),
        out_shape=[jax.ShapeDtypeStruct(shape, BF if bit else F32) for bit in bits],
        compiler_params=pltpu.CompilerParams(vmem_limit_bytes=10 << 20),
        cost_estimate=COST,
        name="input_grad_part",
    )(me, col, w, slope_grad)


def in_vmem(kernel, outs, *args):
    vmem = pl.BlockSpec(memory_space=VMEM)
    return pl.pallas_call(
        kernel,
        in_specs=[vmem] * len(args),
        out_specs=[vmem] * len(outs),
        out_shape=[jax.ShapeDtypeStruct(*x) for x in outs],
        compiler_params=pltpu.CompilerParams(vmem_limit_bytes=10 << 20),
        cost_estimate=SMALL,
        name=kernel.__name__,
    )(*args)


def join(parts):
    def join_parts(*refs):
        row = 0
        for ref in refs[:-1]:
            refs[-1][row : row + ref.shape[0], :] = ref[...]
            row += ref.shape[0]

    shape = (sum(x.shape[0] for x in parts), parts[0].shape[1])
    return in_vmem(join_parts, [(shape, parts[0].dtype)], *parts)[0]


def add_and_split(terms, arrived, keep):
    rows, tokens = terms.shape
    size = keep if keep else rows
    sends = (rows - keep) // size

    def add_stage(terms_ref, *refs):
        arrived_refs, outs = refs[: len(arrived)], refs[len(arrived) :]
        for n, ref in enumerate(outs):
            at = pl.ds(n * size, size)
            total = terms_ref[at, :]
            for more in arrived_refs:
                total = total + more[at, :].astype(F32)
            ref[...] = total.astype(ref.dtype)

    outs = [((keep, tokens), F32)] if keep else []
    outs += [((size, tokens), BF)] * sends
    return in_vmem(add_stage, outs, terms, *arrived)


def add_all(terms, arrived):
    def add_last(*refs):
        total = refs[0][...]
        for ref in refs[1:-1]:
            total = total + ref[...].astype(F32)
        refs[-1][...] = total.astype(BF)

    return in_vmem(add_last, [(terms.shape, BF)], terms, *arrived)[0]


def grads_kernel(groups, pieces, capacity, batch, rows, is_up, *refs):
    tab, count, order, me_ref = refs[:4]
    flat = refs[4 : 4 + sum(pieces)]
    hidden_refs = refs[4 + len(flat) : 4 + len(flat) + groups]
    out, features, tiles_a, tiles_b, *sem = refs[4 + len(flat) + groups :]
    copies = []
    n = 0
    for g in range(groups):
        row = 0
        for _ in range(pieces[g]):
            size = flat[n].shape[0]
            if sem:
                copies.append(
                    pltpu.make_async_copy(
                        flat[n], features.at[g, pl.ds(row, size), :], sem[0].at[n]
                    )
                )
            else:
                features[g, row : row + size, :] = flat[n][...]
            row += size
            n += 1
    for copy in copies:
        copy.start()
    for copy in copies:
        copy.wait()
    low = lax.broadcasted_iota(jnp.int32, (batch, 2 * BS), 1) < BS
    slot = lax.broadcasted_iota(jnp.int32, (batch, 2 * BS), 0)
    live_slots = count[0 if is_up else 1]

    half = features.shape[1] // rows // 2
    far_bits = (half // 2).bit_length() - 1
    per = rows // BS
    per_bits = per.bit_length() - 1

    def place(row, y_first):
        apart = lax.shift_right_logical(row, per_bits) ^ me_ref[0]
        core, y = apart & 1, lax.shift_right_logical(apart, 1) & 1
        z = lax.shift_right_logical(apart, 2)
        spot = core * half + (z * 2 + y if y_first else (y << far_bits) + z)
        return pl.multiple_of(spot * rows + (row & (per - 1)) * BS, BS)

    def multiply(first, tiles):
        for u in range(batch):
            e = jnp.where(first + u < live_slots, tab[first + u], 0)
            row = lax.shift_right_logical(e, KB.bit_length() - 1)
            at = [place(row, False)]
            at += [at[0] if is_up else place(row, True)] * (groups - 1)
            to = pl.multiple_of(order[e] * BS, BS)
            f = jnp.concatenate(
                [features[g, pl.ds(at[g], BS), :] for g in range(groups)], axis=1
            )
            h = jnp.concatenate([ref[pl.ds(to, BS), :] for ref in hidden_refs], axis=1)
            left, right = (f, h) if is_up else (h, f)
            t = lax.dot_general(
                left, right, (((1,), (1,)), ((), ())), preferred_element_type=F32
            )
            tiles[u * PITCH : u * PITCH + BS, :BS] = t

    def flush(first, tiles):
        live = slot + first < live_slots
        for a in range(BS // 2):
            even = tiles[pl.ds(2 * a, batch, stride=PITCH), :]
            odd = pltpu.roll(tiles[pl.ds(2 * a + 1, batch, stride=PITCH), :], BS, 1)
            out[
                pl.ds(pl.multiple_of(first, batch), batch), a * 2 * BS : (a + 1) * 2 * BS
            ] = jnp.where(live, jnp.where(low, even, odd), 0.0).astype(BF)

    steps = capacity // batch

    def body(i, carry):
        first = i * 2 * batch
        multiply(first, tiles_a)
        multiply(first + batch, tiles_b)
        flush(first, tiles_a)
        flush(first + batch, tiles_b)
        return carry

    lax.fori_loop(0, steps // 2, body, 0)
    if steps % 2:
        multiply(capacity - batch, tiles_a)
        flush(capacity - batch, tiles_a)


def owned_grads(tab, count, order, me, features, hiddens, capacity, rows, is_up):
    groups = len(hiddens)
    pieces = tuple(len(group) for group in features)
    batch = GROUP if capacity % GROUP == 0 else 8
    flat = [piece for group in features for piece in group]
    tokens = hiddens[0].shape[1]
    total = sum(piece.shape[0] for piece in features[0])
    small = groups * total * tokens <= 4 << 20
    smem = pl.BlockSpec(memory_space=SMEM)
    vmem = pl.BlockSpec(memory_space=VMEM)
    piece = vmem if small else pl.BlockSpec(memory_space=ANY)
    scratch = [VMEM((groups, total, tokens), BF)] + [VMEM((batch * PITCH, 2 * BS), F32)] * 2
    if not small:
        scratch.append(pltpu.SemaphoreType.DMA((len(flat),)))
    return pl.pallas_call(
        functools.partial(grads_kernel, groups, pieces, capacity, batch, rows, is_up),
        in_specs=[smem] * 4 + [piece] * len(flat) + [vmem] * groups,
        out_specs=vmem,
        out_shape=jax.ShapeDtypeStruct((capacity, BS * BS), BF),
        scratch_shapes=scratch,
        compiler_params=pltpu.CompilerParams(vmem_limit_bytes=(20 if small else 48) << 20),
        cost_estimate=COST,
        name="grads_up" if is_up else "grads_down",
    )(tab, count, order, me, *flat, *hiddens)


def per_device(inputs, cotangent, w_up, w_down, col_up, row_down, owner_up, owner_down):
    rows, tokens = inputs.shape
    blocks = w_up.shape[0]
    groups = lax.axis_size("dp")
    members = lax.axis_size("mp")
    capacity = 5 * blocks // (4 * groups)
    me = lax.axis_index("mp").reshape(1)
    far = members // 4
    after = lax.optimization_barrier
    others = range(1, groups)

    cot_x = [swap(cotangent, "dp", d) for d in others]
    cot_xy = [swap_groups(cotangent, d, 2) for d in others]
    in_parts = [inputs] + [swap(inputs, "mp", 4 * z) for z in range(1, far)]
    up_w = relayout(w_up)
    cot_parts = [cotangent, swap(cotangent, "mp", 4)]
    in_parts, up_w, cot_x, cot_xy, cot_parts, cotangent = after(
        (in_parts, up_w, cot_x, cot_xy, cot_parts, cotangent)
    )
    in_near = join(in_parts)
    in_far = swap(in_near, "mp", 2)
    in_near_o = [swap(in_near, "dp", d) for d in others]
    in_near_b = swap(in_near, "mp", 1)
    cot_parts += [swap(cotangent, "mp", 4 * z) for z in range(2, far)]
    cot_o = [join([x, xy]) for x, xy in zip(cot_x, cot_xy)]
    in_near_b, cot_o = after((in_near_b, cot_o))
    cot_o_1 = [swap(x, "mp", 4) for x in cot_o]
    (hidden,) = hidden_sum(
        rows, True, me, col_up, up_w, [in_near, in_near_b], [(0, 0), (1, 0)]
    )
    hidden, w_down, owner_up, owner_down = after((hidden, w_down, owner_up, owner_down))
    down_w = relayout(w_down)
    up_tab, down_tab, counts = slots(
        lax.axis_index("dp").reshape(1), owner_up[:, 0], owner_down[:, 0]
    )
    cot_o, cot_o_1, in_near_o, cot_parts, in_far, hidden, down_w, up_tab = after(
        (cot_o, cot_o_1, in_near_o, cot_parts, in_far, hidden, down_w, up_tab)
    )
    cot_near = join(cot_parts)
    cot_far = swap(cot_near, "mp", 2)
    cot_near_b = swap(cot_near, "mp", 1)
    in_far_b = swap(in_far, "mp", 1)
    in_far_o = [swap(in_far, "dp", d) for d in others]
    cot_o_z = [[swap(x, "mp", 4 * z) for z in range(2, far)] for x in cot_o]
    (upper,) = hidden_sum(
        rows, False, me, row_down, down_w, [cot_near, cot_near_b], [(0, 0), (1, 0)]
    )
    active, slope = hidden_sum(
        rows, True, me, col_up, up_w, [in_far, in_far_b], [(0, far), (1, far)], hidden, True
    )
    early = [x[: far // 2 - 1] for x in cot_o_z]
    cot_far, slope, upper, in_far_o, early = after((cot_far, slope, upper, in_far_o, early))
    cot_far_b = swap(cot_far, "mp", 1)
    (upper,) = hidden_sum(rows, False, me, row_down, down_w, [cot_far], [(0, far)], upper)
    slope_grad, sent = hidden_sum(
        rows, False, me, row_down, down_w, [cot_far_b], [(1, far)], upper, True,
        slope, (col_up, up_w),
    )
    slope_grad_o = [swap(slope_grad, "dp", d) for d in others]

    part = functools.partial(input_grad_part, rows)
    arrived = swap(sent, "mp", 1)
    (terms,) = part(far, (0,), me, col_up, up_w, slope_grad)
    (sent,) = add_and_split(terms, [arrived], 0)
    arrived = swap(sent, "mp", 2)
    sent, near_slope_grad, near_active = after((sent, slope_grad, active))
    active_o = [swap(near_active, "dp", d) for d in others]
    sent_b, terms = part(0, (1, 0), me, col_up, up_w, near_slope_grad)
    arrived_b = swap(sent_b, "mp", 1)
    in_near_o_b = [swap(x, "mp", 1) for x in in_near_o]
    in_far_o_b = [swap(x, "mp", 1) for x in in_far_o]
    in_all = [[in_near, in_far, in_near_b, in_far_b]]
    in_all += [list(x) for x in zip(in_near_o, in_far_o, in_near_o_b, in_far_o_b)]
    late = [x[far // 2 - 1 :] for x in cot_o_z]
    arrived, late, slope_grad_o, terms = after((arrived, late, slope_grad_o, terms))
    cot_o = [
        [x, x_1] + near + rest for x, x_1, near, rest in zip(cot_o, cot_o_1, early, late)
    ]
    terms, *sent = add_and_split(terms, [arrived, arrived_b], rows)
    pieces = [swap(x, "mp", 4 * z + 4) for z, x in enumerate(sent)]
    cot_o_b = [[swap(piece, "mp", 1) for piece in x] for x in cot_o]
    cot_all = [[cot_near, cot_far, cot_near_b, cot_far_b]]
    cot_all += [x + x_b for x, x_b in zip(cot_o, cot_o_b)]
    grad_up = owned_grads(
        up_tab, counts, col_up, me, in_all, [slope_grad] + slope_grad_o, capacity, rows, True
    )
    grad_down = owned_grads(
        down_tab, counts, row_down, me, cot_all, [active] + active_o, capacity, rows, False
    )
    pieces, grad_up, grad_down = after((pieces, grad_up, grad_down))
    return active, add_all(terms, pieces), grad_up, grad_down


def solution(mesh):
    placed = (
        P("mp", "dp"),
        P("mp", "dp"),
        P("mp", None),
        P("mp", None),
        P("mp"),
        P("mp"),
        P("mp", None),
        P("mp", None),
    )
    return jax.shard_map(
        per_device,
        mesh=mesh,
        in_specs=placed,
        out_specs=(P("mp", "dp"), P("mp", "dp"), P(("dp", "mp"), None), P(("dp", "mp"), None)),
        check_vma=False,
    )
```

```python
import functools
import jax
import jax.numpy as jnp
from jax import lax
from jax.experimental import pallas as pl
from jax.experimental.pallas import tpu as pltpu
from jax.sharding import PartitionSpec as P

BS = 64
FBLK = 16
KB = 2
GROUP = 16
RELAYOUT = 64
PITCH = BS + 1
VMEM = pltpu.VMEM
SMEM = pltpu.SMEM
ANY = pl.ANY
BF = jnp.bfloat16
F32 = jnp.float32
COST = pl.CostEstimate(flops=1 << 29, bytes_accessed=6 << 20, transcendentals=0)
SMALL = pl.CostEstimate(flops=1000, bytes_accessed=1 << 20, transcendentals=0)


def swap(value, axis, mask):
    size = lax.axis_size(axis)
    return lax.ppermute(value, axis, [(i, i ^ mask) for i in range(size)])


def swap_groups(value, group_mask, mask):
    groups, size = lax.axis_size("dp"), lax.axis_size("mp")
    pairs = [
        (g * size + i, (g ^ group_mask) * size + (i ^ mask))
        for g in range(groups)
        for i in range(size)
    ]
    return lax.ppermute(value, ("dp", "mp"), pairs)


def relayout_kernel(blocks, src, out, tall):
    lane = lax.broadcasted_iota(jnp.int32, (BS, 2 * BS), 1) < BS
    even = lax.broadcasted_iota(jnp.int32, (blocks, 2 * BS), 0) % 2 == 0

    def body(i, carry):
        rows = pl.ds(pl.multiple_of(i * blocks, blocks), blocks)
        for a in range(BS // 2):
            tile = src[rows, a * 2 * BS : (a + 1) * 2 * BS].astype(F32)
            turned = pltpu.roll(tile, BS, 1)
            tall[pl.ds(2 * a, blocks, stride=PITCH), :] = jnp.where(even, tile, turned)
            tall[pl.ds(2 * a + 1, blocks, stride=PITCH), :] = jnp.where(even, turned, tile)
        for r in range(blocks // KB):
            first = tall[2 * r * PITCH : 2 * r * PITCH + BS, :]
            second = tall[(2 * r + 1) * PITCH : (2 * r + 1) * PITCH + BS, :]
            at = pl.multiple_of(i * (blocks // KB) * BS + r * BS, BS)
            out[pl.ds(at, BS), :] = jnp.where(lane, first, second).astype(BF)
        return carry

    lax.fori_loop(0, src.shape[0] // blocks, body, 0)


def relayout(w):
    vmem = pl.BlockSpec(memory_space=VMEM)
    return pl.pallas_call(
        functools.partial(relayout_kernel, RELAYOUT),
        in_specs=[vmem],
        out_specs=vmem,
        out_shape=jax.ShapeDtypeStruct((w.shape[0] * BS // KB, KB * BS), BF),
        scratch_shapes=[VMEM((RELAYOUT * PITCH, 2 * BS), F32)],
        compiler_params=pltpu.CompilerParams(vmem_limit_bytes=16 << 20),
        cost_estimate=COST,
        name="relayout",
    )(w)


def slots_kernel(me_ref, up_ref, down_ref, up_tab, down_tab, counts):
    group = me_ref[0]
    total = up_ref.shape[0]

    def body(i, carry):
        a, b = carry
        for u in range(8):
            e = i * 8 + u
            up_tab[a] = e
            down_tab[b] = e
            a = a + (up_ref[e] == group).astype(jnp.int32)
            b = b + (down_ref[e] == group).astype(jnp.int32)
        return a, b

    a, b = lax.fori_loop(0, total // 8, body, (jnp.int32(0), jnp.int32(0)))
    counts[0] = a
    counts[1] = b


def slots(group, owner_up, owner_down):
    total = owner_up.shape[0]
    shape = jax.ShapeDtypeStruct((total + 8,), jnp.int32)
    spec = pl.BlockSpec(memory_space=SMEM)
    return pl.pallas_call(
        slots_kernel,
        in_specs=[spec] * 3,
        out_specs=[spec] * 3,
        out_shape=[shape, shape, jax.ShapeDtypeStruct((2,), jnp.int32)],
        cost_estimate=COST,
        name="slots",
    )(group, owner_up, owner_down)


def gelu_slope(value):
    scale = 0.7978845608028654
    cubic = 0.044715
    inner = scale * (value + cubic * value * value * value)
    tanh_part = jnp.tanh(inner)
    gate = 0.5 * (1.0 + tanh_part)
    slope = gate + 0.5 * value * (1.0 - tanh_part * tanh_part) * scale * (
        1.0 + 3.0 * cubic * value * value
    )
    return value * gate, slope


def source(me, i, far):
    return me ^ ((i // far) * 2 + (i % far) * 4)


def add_blocks(me_ref, where_ref, w_ref, x_refs, starts, acc, rows, is_up):
    far = w_ref.shape[0] // rows // 4
    per = rows // BS
    zero = jnp.zeros((BS, acc.shape[1]), BF)
    width = acc.shape[1]
    for x_ref, (bit, skip) in zip(x_refs, starts):

        def body(i, carry, x_ref=x_ref, bit=bit, skip=skip):
            start = source(me_ref[0] ^ bit, skip + i, far) * per
            for rr in range(per):
                r = start + rr
                w = w_ref[pl.ds(pl.multiple_of(r * BS, BS), BS), :]
                x = x_ref[pl.ds(pl.multiple_of(i * rows + rr * BS, BS), BS), :]
                if is_up:
                    t = lax.dot_general(
                        w, x, (((0,), (0,)), ((), ())), preferred_element_type=F32
                    )
                    parts = [t[q * BS : (q + 1) * BS, :] for q in range(KB)]
                else:
                    right = jnp.concatenate(
                        [
                            jnp.concatenate([x, zero], axis=1),
                            jnp.concatenate([zero, x], axis=1),
                        ],
                        axis=0,
                    )
                    t = jnp.dot(w, right, preferred_element_type=F32)
                    parts = [t[:, q * width : (q + 1) * width] for q in range(KB)]
                for q in range(KB):
                    to = pl.ds(pl.multiple_of(where_ref[KB * r + q] * BS, BS), BS)
                    acc[to, :] += parts[q]
            return carry

        lax.fori_loop(0, x_ref.shape[0] // rows, body, 0)


def hidden_kernel(rows, is_up, starts, first, last, *refs):
    me_ref, where_ref, w_ref = refs[:3]
    x_refs = refs[3 : 3 + len(starts)]
    rest = list(refs[3 + len(starts) :])
    acc_in = None if first else rest.pop(0)
    if not last:
        (acc,) = rest
    elif is_up:
        active, slope_ref, acc = rest
    else:
        slope_ref, col_ref, up_ref, slope_grad, sent, acc = rest
    acc[...] = jnp.zeros_like(acc) if first else acc_in[...]
    add_blocks(me_ref, where_ref, w_ref, x_refs, starts, acc, rows, is_up)
    if last:
        ff = acc.shape[0]

        def body(i, carry):
            here = pl.ds(pl.multiple_of(i * BS, BS), BS)
            if is_up:
                value, slope = gelu_slope(acc[here, :])
                active[here, :] = value.astype(BF)
                slope_ref[here, :] = slope
            else:
                slope_grad[here, :] = (acc[here, :] * slope_ref[here, :]).astype(BF)
            return carry

        lax.fori_loop(0, ff // BS, body, 0)
        if not is_up:
            skip = up_ref.shape[0] // rows // 4
            input_grad_kernel(rows, skip, (1,), me_ref, col_ref, up_ref, slope_grad, sent)


def hidden_sum(rows, is_up, me, where, w, pieces, starts, acc=None, last=False, slope=None, up=()):
    ff, tokens = FBLK * BS, pieces[0].shape[1]
    smem = pl.BlockSpec(memory_space=SMEM)
    vmem = pl.BlockSpec(memory_space=VMEM)
    more = [x for x in (acc, slope) if x is not None]
    whole, kept = jax.ShapeDtypeStruct((ff, tokens), F32), jax.ShapeDtypeStruct((ff, tokens), BF)
    if not last:
        outs = [whole]
    elif is_up:
        outs = [kept, whole]
    else:
        outs = [kept, jax.ShapeDtypeStruct((w.shape[0] // 4, tokens), BF)]
    return pl.pallas_call(
        functools.partial(hidden_kernel, rows, is_up, tuple(starts), acc is None, last),
        in_specs=[smem, smem] + [vmem] * (1 + len(pieces) + len(more)) + [smem, vmem][: len(up)],
        out_specs=[vmem] * len(outs),
        out_shape=outs,
        scratch_shapes=[VMEM((ff, tokens), F32)] if last else [],
        compiler_params=pltpu.CompilerParams(vmem_limit_bytes=12 << 20),
        cost_estimate=COST,
        name=("hidden" if is_up else "upper") + ("_last" if last else ""),
    )(me, where, w, *pieces, *more, *up)


def input_grad_kernel(rows, skip, bits, me_ref, col_ref, w_ref, s_ref, *outs):
    per = rows // BS
    chunks = outs[0].shape[0] // rows

    def one(i, bit, out):
        start = source(me_ref[0] ^ bit, skip + i, chunks) * per
        for rr in range(per):
            r = start + rr
            w = w_ref[pl.ds(pl.multiple_of(r * BS, BS), BS), :]
            parts = [
                s_ref[pl.ds(pl.multiple_of(col_ref[KB * r + q] * BS, BS), BS), :]
                for q in range(KB)
            ]
            t = jnp.dot(w, jnp.concatenate(parts, axis=0), preferred_element_type=F32)
            out[pl.ds(pl.multiple_of(i * rows + rr * BS, BS), BS), :] = t.astype(out.dtype)

    def body(i, carry):
        for bit, out in zip(bits, outs):
            one(i, bit, out)
        return carry

    lax.fori_loop(0, chunks, body, 0)


def input_grad_part(rows, skip, bits, me, col, w, slope_grad):
    smem = pl.BlockSpec(memory_space=SMEM)
    vmem = pl.BlockSpec(memory_space=VMEM)
    shape = (w.shape[0] // 4, slope_grad.shape[1])
    return pl.pallas_call(
        functools.partial(input_grad_kernel, rows, skip, bits),
        in_specs=[smem, smem, vmem, vmem],
        out_specs=[vmem] * len(bits),
        out_shape=[jax.ShapeDtypeStruct(shape, BF if bit else F32) for bit in bits],
        compiler_params=pltpu.CompilerParams(vmem_limit_bytes=10 << 20),
        cost_estimate=COST,
        name="input_grad_part",
    )(me, col, w, slope_grad)


def in_vmem(kernel, outs, *args):
    vmem = pl.BlockSpec(memory_space=VMEM)
    return pl.pallas_call(
        kernel,
        in_specs=[vmem] * len(args),
        out_specs=[vmem] * len(outs),
        out_shape=[jax.ShapeDtypeStruct(*x) for x in outs],
        compiler_params=pltpu.CompilerParams(vmem_limit_bytes=10 << 20),
        cost_estimate=SMALL,
        name=kernel.__name__,
    )(*args)


def join(parts):
    def join_parts(*refs):
        row = 0
        for ref in refs[:-1]:
            refs[-1][row : row + ref.shape[0], :] = ref[...]
            row += ref.shape[0]

    shape = (sum(x.shape[0] for x in parts), parts[0].shape[1])
    return in_vmem(join_parts, [(shape, parts[0].dtype)], *parts)[0]


def add_and_split(terms, arrived, keep):
    rows, tokens = terms.shape
    size = keep if keep else rows
    sends = (rows - keep) // size

    def add_stage(terms_ref, *refs):
        arrived_refs, outs = refs[: len(arrived)], refs[len(arrived) :]
        for n, ref in enumerate(outs):
            at = pl.ds(n * size, size)
            total = terms_ref[at, :]
            for more in arrived_refs:
                total = total + more[at, :].astype(F32)
            ref[...] = total.astype(ref.dtype)

    outs = [((keep, tokens), F32)] if keep else []
    outs += [((size, tokens), BF)] * sends
    return in_vmem(add_stage, outs, terms, *arrived)


def add_all(terms, arrived):
    def add_last(*refs):
        total = refs[0][...]
        for ref in refs[1:-1]:
            total = total + ref[...].astype(F32)
        refs[-1][...] = total.astype(BF)

    return in_vmem(add_last, [(terms.shape, BF)], terms, *arrived)[0]


def grads_kernel(groups, pieces, capacity, batch, rows, is_up, *refs):
    tab, count, order, me_ref = refs[:4]
    flat = refs[4 : 4 + sum(pieces)]
    hidden_refs = refs[4 + len(flat) : 4 + len(flat) + groups]
    out, features, tiles_a, tiles_b, *sem = refs[4 + len(flat) + groups :]
    copies = []
    n = 0
    for g in range(groups):
        row = 0
        for _ in range(pieces[g]):
            size = flat[n].shape[0]
            if sem:
                copies.append(
                    pltpu.make_async_copy(
                        flat[n], features.at[g, pl.ds(row, size), :], sem[0].at[n]
                    )
                )
            else:
                features[g, row : row + size, :] = flat[n][...]
            row += size
            n += 1
    for copy in copies:
        copy.start()
    for copy in copies:
        copy.wait()
    low = lax.broadcasted_iota(jnp.int32, (batch, 2 * BS), 1) < BS
    slot = lax.broadcasted_iota(jnp.int32, (batch, 2 * BS), 0)
    live_slots = count[0 if is_up else 1]

    half = features.shape[1] // rows // 2
    far_bits = (half // 2).bit_length() - 1
    per = rows // BS
    per_bits = per.bit_length() - 1

    def place(row, y_first):
        apart = lax.shift_right_logical(row, per_bits) ^ me_ref[0]
        core, y = apart & 1, lax.shift_right_logical(apart, 1) & 1
        z = lax.shift_right_logical(apart, 2)
        spot = core * half + (z * 2 + y if y_first else (y << far_bits) + z)
        return pl.multiple_of(spot * rows + (row & (per - 1)) * BS, BS)

    def multiply(first, tiles):
        for u in range(batch):
            e = jnp.where(first + u < live_slots, tab[first + u], 0)
            row = lax.shift_right_logical(e, KB.bit_length() - 1)
            at = [place(row, False)]
            at += [at[0] if is_up else place(row, True)] * (groups - 1)
            to = pl.multiple_of(order[e] * BS, BS)
            f = jnp.concatenate(
                [features[g, pl.ds(at[g], BS), :] for g in range(groups)], axis=1
            )
            h = jnp.concatenate([ref[pl.ds(to, BS), :] for ref in hidden_refs], axis=1)
            left, right = (f, h) if is_up else (h, f)
            t = lax.dot_general(
                left, right, (((1,), (1,)), ((), ())), preferred_element_type=F32
            )
            tiles[u * PITCH : u * PITCH + BS, :BS] = t

    def flush(first, tiles):
        live = slot + first < live_slots
        for a in range(BS // 2):
            even = tiles[pl.ds(2 * a, batch, stride=PITCH), :]
            odd = pltpu.roll(tiles[pl.ds(2 * a + 1, batch, stride=PITCH), :], BS, 1)
            out[
                pl.ds(pl.multiple_of(first, batch), batch), a * 2 * BS : (a + 1) * 2 * BS
            ] = jnp.where(live, jnp.where(low, even, odd), 0.0).astype(BF)

    steps = capacity // batch

    def body(i, carry):
        first = i * 2 * batch
        multiply(first, tiles_a)
        multiply(first + batch, tiles_b)
        flush(first, tiles_a)
        flush(first + batch, tiles_b)
        return carry

    lax.fori_loop(0, steps // 2, body, 0)
    if steps % 2:
        multiply(capacity - batch, tiles_a)
        flush(capacity - batch, tiles_a)


def owned_grads(tab, count, order, me, features, hiddens, capacity, rows, is_up):
    groups = len(hiddens)
    pieces = tuple(len(group) for group in features)
    batch = GROUP if capacity % GROUP == 0 else 8
    flat = [piece for group in features for piece in group]
    tokens = hiddens[0].shape[1]
    total = sum(piece.shape[0] for piece in features[0])
    small = groups * total * tokens <= 4 << 20
    smem = pl.BlockSpec(memory_space=SMEM)
    vmem = pl.BlockSpec(memory_space=VMEM)
    piece = vmem if small else pl.BlockSpec(memory_space=ANY)
    scratch = [VMEM((groups, total, tokens), BF)] + [VMEM((batch * PITCH, 2 * BS), F32)] * 2
    if not small:
        scratch.append(pltpu.SemaphoreType.DMA((len(flat),)))
    return pl.pallas_call(
        functools.partial(grads_kernel, groups, pieces, capacity, batch, rows, is_up),
        in_specs=[smem] * 4 + [piece] * len(flat) + [vmem] * groups,
        out_specs=vmem,
        out_shape=jax.ShapeDtypeStruct((capacity, BS * BS), BF),
        scratch_shapes=scratch,
        compiler_params=pltpu.CompilerParams(vmem_limit_bytes=(20 if small else 48) << 20),
        cost_estimate=COST,
        name="grads_up" if is_up else "grads_down",
    )(tab, count, order, me, *flat, *hiddens)


def per_device(inputs, cotangent, w_up, w_down, col_up, row_down, owner_up, owner_down):
    rows, tokens = inputs.shape
    blocks = w_up.shape[0]
    groups = lax.axis_size("dp")
    members = lax.axis_size("mp")
    capacity = 5 * blocks // (4 * groups)
    me = lax.axis_index("mp").reshape(1)
    far = members // 4
    after = lax.optimization_barrier
    others = range(1, groups)

    cot_x = [swap(cotangent, "dp", d) for d in others]
    cot_xy = [swap_groups(cotangent, d, 2) for d in others]
    in_parts = [inputs] + [swap(inputs, "mp", 4 * z) for z in range(1, far)]
    up_w = relayout(w_up)
    cot_parts = [cotangent, swap(cotangent, "mp", 4)]
    in_parts, up_w, cot_x, cot_xy, cot_parts, cotangent = after(
        (in_parts, up_w, cot_x, cot_xy, cot_parts, cotangent)
    )
    in_near = join(in_parts)
    in_far = swap(in_near, "mp", 2)
    in_near_o = [swap(in_near, "dp", d) for d in others]
    in_near_b = swap(in_near, "mp", 1)
    cot_parts += [swap(cotangent, "mp", 4 * z) for z in range(2, far)]
    cot_o = [join([x, xy]) for x, xy in zip(cot_x, cot_xy)]
    cot_o_1 = [swap(x, "mp", 4) for x in cot_o]
    (hidden,) = hidden_sum(
        rows, True, me, col_up, up_w, [in_near, in_near_b], [(0, 0), (1, 0)]
    )
    hidden, w_down, owner_up, owner_down = after((hidden, w_down, owner_up, owner_down))
    down_w = relayout(w_down)
    up_tab, down_tab, counts = slots(
        lax.axis_index("dp").reshape(1), owner_up[:, 0], owner_down[:, 0]
    )
    cot_o, cot_o_1, in_near_o, cot_parts, in_far, hidden, down_w, up_tab = after(
        (cot_o, cot_o_1, in_near_o, cot_parts, in_far, hidden, down_w, up_tab)
    )
    cot_near = join(cot_parts)
    cot_far = swap(cot_near, "mp", 2)
    cot_near_b = swap(cot_near, "mp", 1)
    in_far_b = swap(in_far, "mp", 1)
    in_far_o = [swap(in_far, "dp", d) for d in others]
    early = [[swap(x, "mp", 4 * z) for z in range(2, far - 1)] for x in cot_o]
    (upper,) = hidden_sum(
        rows, False, me, row_down, down_w, [cot_near, cot_near_b], [(0, 0), (1, 0)]
    )
    active, slope = hidden_sum(
        rows, True, me, col_up, up_w, [in_far, in_far_b], [(0, far), (1, far)], hidden, True
    )
    cot_far, slope, upper, in_far_o, early = after((cot_far, slope, upper, in_far_o, early))
    cot_far_b = swap(cot_far, "mp", 1)
    (upper,) = hidden_sum(rows, False, me, row_down, down_w, [cot_far], [(0, far)], upper)
    slope_grad, sent = hidden_sum(
        rows, False, me, row_down, down_w, [cot_far_b], [(1, far)], upper, True,
        slope, (col_up, up_w),
    )
    slope_grad_o = [swap(slope_grad, "dp", d) for d in others]

    part = functools.partial(input_grad_part, rows)
    arrived = swap(sent, "mp", 1)
    (terms,) = part(far, (0,), me, col_up, up_w, slope_grad)
    (sent,) = add_and_split(terms, [arrived], 0)
    arrived = swap(sent, "mp", 2)
    sent, near_slope_grad, near_active, near_cot_o = after((sent, slope_grad, active, cot_o))
    late = [[swap(x, "mp", 4 * (far - 1))] for x in near_cot_o]
    active_o = [swap(near_active, "dp", d) for d in others]
    sent_b, terms = part(0, (1, 0), me, col_up, up_w, near_slope_grad)
    arrived_b = swap(sent_b, "mp", 1)
    in_near_o_b = [swap(x, "mp", 1) for x in in_near_o]
    in_far_o_b = [swap(x, "mp", 1) for x in in_far_o]
    in_all = [[in_near, in_far, in_near_b, in_far_b]]
    in_all += [list(x) for x in zip(in_near_o, in_far_o, in_near_o_b, in_far_o_b)]
    arrived, late, slope_grad_o, terms = after((arrived, late, slope_grad_o, terms))
    cot_o = [
        [x, x_1] + near + rest for x, x_1, near, rest in zip(cot_o, cot_o_1, early, late)
    ]
    terms, *sent = add_and_split(terms, [arrived, arrived_b], rows)
    pieces = [swap(x, "mp", 4 * z + 4) for z, x in enumerate(sent)]
    cot_o_b = [[swap(piece, "mp", 1) for piece in x] for x in cot_o]
    cot_all = [[cot_near, cot_far, cot_near_b, cot_far_b]]
    cot_all += [x + x_b for x, x_b in zip(cot_o, cot_o_b)]
    grad_up = owned_grads(
        up_tab, counts, col_up, me, in_all, [slope_grad] + slope_grad_o, capacity, rows, True
    )
    grad_down = owned_grads(
        down_tab, counts, row_down, me, cot_all, [active] + active_o, capacity, rows, False
    )
    pieces, grad_up, grad_down = after((pieces, grad_up, grad_down))
    return active, add_all(terms, pieces), grad_up, grad_down


def solution(mesh):
    placed = (
        P("mp", "dp"),
        P("mp", "dp"),
        P("mp", None),
        P("mp", None),
        P("mp"),
        P("mp"),
        P("mp", None),
        P("mp", None),
    )
    return jax.shard_map(
        per_device,
        mesh=mesh,
        in_specs=placed,
        out_specs=(P("mp", "dp"), P("mp", "dp"), P(("dp", "mp"), None), P(("dp", "mp"), None)),
        check_vma=False,
    )
```
